32 devices in a mesh: ctx: 8 (over y, x, core), tp: 4 (over z).
Axes of the slice: x: 2, y: 2, z: 4, core: 2. Of those that a mesh axis runs over, the one named last changes fastest.
Arguments:
- query_mr: bfloat16 [2048, 8192], P('ctx', 'tp'), may hold values from -6 to 6
- key_mr: bfloat16 [2048, 8192], P('ctx', 'tp'), may hold values from -6 to 6
- value_mr: bfloat16 [2048, 8192], P('ctx', 'tp'), may hold values from -6 to 6
- query_li: bfloat16 [2048, 8192], P('ctx', 'tp'), may hold values from -6 to 6
- key_li: bfloat16 [2048, 8192], P('ctx', 'tp'), may hold values from -6 to 6
- cotangent: bfloat16 [2048, 8192], P('ctx', 'tp'), may hold values from -6 to 6
- mr_taps: float32 [128, 8192], P(None, 'tp'), may hold values from -0.5 to 0.5
- decay_rates: float32 [8], replicated, may hold values from 4.8828126e-05 to 0.03
- residues: float32 [8, 8192], P(None, 'tp'), may hold values from -2 to 2
Outputs:
- grad_query_mr: bfloat16 [2048, 8192], P('ctx', 'tp')
- grad_key_mr: bfloat16 [2048, 8192], P('ctx', 'tp')
- grad_value_mr: bfloat16 [2048, 8192], P('ctx', 'tp')
- grad_query_li: bfloat16 [2048, 8192], P('ctx', 'tp')
- grad_key_li: bfloat16 [2048, 8192], P('ctx', 'tp')
- grad_taps: float32 [128, 8192], P(None, 'tp')
- grad_residues: float32 [8, 8192], P(None, 'tp')
The draws below stay inside these ranges and needn't reach their ends.
All inputs are finite; a program needn't handle non-finite values.
Results may differ from the reference program's by a relative error of at most 0.001.
Values may be sent and summed in bfloat16 or wider, within the bound.
A program may use at most 128 MiB of HBM per device.

```python
import math
import jax
import jax.numpy as jnp
from jax import lax

D = 8192
TAPS = 128
MODES = 8
SEQ = 2048


def levels(key, dims, pieces, least, largest):
    gain = 1.0
    for axis_at, shards_of in pieces:
        draws = jax.random.uniform(jax.random.fold_in(jax.random.fold_in(key, 6), axis_at), (shards_of,), jnp.float32, least / len(pieces), largest / len(pieces))
        gain = gain * jnp.repeat(jnp.exp(draws), dims[axis_at] // shards_of).reshape((-1,) + (1,) * (len(dims) - 1 - axis_at))
    return gain


def gaussian(stream_key, extent, deviation, bound, split=(), held_as=jnp.bfloat16):
    result = jax.random.normal(stream_key, extent, jnp.float32) * deviation
    if len(split) > 0:
        result = levels(stream_key, extent, split, -0.22, 0.18) * result
    return jnp.clip(result, min=-bound, max=bound).astype(held_as)


def setup_inputs(seed: int = 0) -> dict:
    splits = jax.random.split(jax.random.key(seed), 10)
    query_mr = gaussian(splits[0], (SEQ, D), 1.0, 6.0, ((0, 8), (1, 4)))
    key_mr = gaussian(splits[1], (SEQ, D), 1.0, 6.0, ((0, 8), (1, 4)))
    value_mr = gaussian(splits[2], (SEQ, D), 1.0, 6.0, ((0, 8), (1, 4)))
    query_li = gaussian(splits[3], (SEQ, D), 1.0, 6.0, ((0, 8), (1, 4)))
    key_li = gaussian(splits[4], (SEQ, D), 1.0, 6.0, ((0, 8), (1, 4)))
    cotangent = gaussian(splits[5], (SEQ, D), 1.0, 6.0, ((0, 8), (1, 4)))
    mr_taps = gaussian(splits[6], (TAPS, D), TAPS ** -0.5, 0.5, ((1, 4),), jnp.float32)
    decay_rates = jnp.clip(jnp.exp(jax.random.uniform(splits[7], (MODES,), jnp.float32, math.log(4.882812572759576e-05), math.log(0.03))), 4.882812572759576e-05, 0.03)
    residues = gaussian(splits[8], (MODES, D), MODES ** -0.5, 2.0, ((1, 4),), jnp.float32)
    return {"query_mr": query_mr, "key_mr": key_mr, "value_mr": value_mr, "query_li": query_li, "key_li": key_li, "cotangent": cotangent, "mr_taps": mr_taps, "decay_rates": decay_rates, "residues": residues}


highest = lax.Precision.HIGHEST

def causal(signal, kernel, length):
    total = 2 * length
    spectrum = jnp.fft.rfft(signal, total, axis=0) * jnp.fft.rfft(kernel, total, axis=0)
    return jnp.fft.irfft(spectrum, total, axis=0)[:length]

def later_sum(signal, kernel, length):
    return causal(signal[::-1], kernel, length)[::-1]

def lagged(first, second, length):
    return causal(first, second[::-1], length)[::-1]

def reference(query_mr, key_mr, value_mr, query_li, key_li, cotangent, mr_taps, decay_rates, residues):
    length = SEQ
    group_cols = math.gcd(D, 256)
    places = jnp.arange(length, dtype=jnp.float32)
    decay_table = jnp.sqrt(-jnp.expm1(-2.0 * decay_rates))[None, :] * jnp.exp(-places[:, None] * decay_rates[None, :])

    def one_group(index):
        start = index * group_cols

        def columns(array):
            return lax.dynamic_slice_in_dim(array, start, group_cols, 1).astype(jnp.float32)
        taps_block = jnp.concatenate([columns(mr_taps), jnp.zeros((length - TAPS, group_cols), jnp.float32)], 0)
        long_filter = jnp.dot(decay_table, columns(residues), precision=highest)
        key_first = columns(key_mr)
        value_first = columns(value_mr)
        mixed_in = key_first * value_first
        mr_conv = causal(mixed_in, taps_block, length)
        mr_out = columns(query_mr) * mr_conv
        key_second = columns(key_li)
        cotan = columns(cotangent)
        li_input = key_second * mr_out
        li_cotan = cotan * columns(query_li)
        li_conv = causal(li_input, long_filter, length)
        li_back = later_sum(li_cotan, long_filter, length)
        residue_sum = jnp.dot(decay_table.T, lagged(li_input, li_cotan, length), precision=highest)
        grad_query_li = (cotan * li_conv).astype(jnp.bfloat16)
        grad_key_li = (mr_out * li_back).astype(jnp.bfloat16)
        mr_grad = cotan + key_second * li_back
        grad_query_mr = (mr_grad * mr_conv).astype(jnp.bfloat16)
        mr_cotan = mr_grad * columns(query_mr)
        mixed_grad = later_sum(mr_cotan, taps_block, length)
        grad_key_mr = (mixed_grad * value_first).astype(jnp.bfloat16)
        grad_value_mr = (mixed_grad * key_first).astype(jnp.bfloat16)
        tap_sum = lagged(mixed_in, mr_cotan, length)[:TAPS]
        return (grad_query_mr, grad_key_mr, grad_value_mr, grad_query_li, grad_key_li, tap_sum, residue_sum)
    results = lax.map(one_group, jnp.arange(D // group_cols, dtype=jnp.int32))

    def joined(array):
        return jnp.moveaxis(array, 0, 1).reshape(array.shape[1], D)
    factor = 1.0 / math.sqrt(length)
    return (joined(results[0]), joined(results[1]), joined(results[2]), joined(results[3]), joined(results[4]), joined(results[5]) * factor, joined(results[6]) * factor)
```

```python
import math

import numpy as np
import ml_dtypes
import jax
import jax.numpy as jnp
from jax import lax
from jax.experimental import pallas as pl
from jax.experimental.pallas import tpu as pltpu
from jax.sharding import PartitionSpec as P

f32, bf16 = jnp.float32, jnp.bfloat16
WIDE = 256


def tables(taps):
    size, half = 2 * taps, taps // 2
    order = np.concatenate([np.arange(0, taps, 2), np.arange(1, taps, 2)])
    angle = (2.0 * np.pi / size) * (order[:, None] + 0.5) * np.arange(size)[None, :]
    full = np.concatenate([np.cos(angle), -np.sin(angle)], 0)

    def three(table):
        hi = table.astype(ml_dtypes.bfloat16)
        lo = (table - hi.astype(np.float64)).astype(ml_dtypes.bfloat16)
        return np.concatenate([hi, hi, lo], 1)

    return (
        three(full),
        three(full[:, :taps]),
        three(full[:, :taps].T),
        three(full[:, taps:].T),
    )


def split(x):
    hi = x.astype(bf16)
    return hi, (x - hi.astype(f32)).astype(bf16)


def three(x):
    hi, lo = split(x)
    return jnp.concatenate([hi, lo, hi], 0)


def three_small(x):
    hi = x.astype(bf16).astype(f32)
    return jnp.concatenate([hi, x - hi, hi, jnp.zeros_like(x)], 0).astype(bf16)


def three_lanes(x):
    hi, lo = split(x)
    return jnp.concatenate([hi, hi, lo], 1)


def dot(a, b):
    return jnp.dot(a, b, preferred_element_type=f32)


def parts_of(z):
    n = z.shape[0] // 2
    return z[:n], z[n:]


def cmul(a, b):
    (ar, ai), (br, bi) = parts_of(a), parts_of(b)
    return jnp.concatenate([ar * br - ai * bi, ar * bi + ai * br], 0)


def cmul_conj(a, b):
    (ar, ai), (br, bi) = parts_of(a), parts_of(b)
    return jnp.concatenate([ar * br + ai * bi, ar * bi - ai * br], 0)


def turned(z):
    q = z.shape[0] // 4
    return jnp.concatenate([z[2 * q : 3 * q], -z[3 * q :], -z[:q], z[q : 2 * q]], 0)


def add_turned(y, z):
    q = z.shape[0] // 4
    return jnp.concatenate(
        [
            y[:q] + z[2 * q : 3 * q],
            y[q : 2 * q] - z[3 * q :],
            y[2 * q : 3 * q] - z[:q],
            y[3 * q :] + z[q : 2 * q],
        ],
        0,
    )


def conj_turned(w, z):
    n = w.shape[0] // 2
    h = n // 2
    wr, wi, zr, zi = w[:n], w[n:], z[:n], z[n:]
    re = wr * zi - wi * zr
    im = wr * zr + wi * zi
    return jnp.concatenate([re[:h], -re[h:], -im[:h], im[h:]], 0)


def kernel(
    size, factor,
    q1_in, k1_in, v1_in, q2_in, k2_in, co_in, taps_in, rates, res_in, tf_in, th_in, tn_in, ti_in,
    gq1_out, gk1_out, gv1_out, gq2_out, gk2_out, taps_out, res_out,
    q1, k1, v1, q2, k2, co, taps, res, tf, thr, thf, tn, ti,
    rise_t, ms_t, mst_t, lead_t, tail_t,
    lspec, kback, tspec, fspec, wone, mr_one, lback, lconv, ctail,
    gq1, gk1, gv1, gq2, gk2, taps_st, res_st,
    bstate, bslots, fstate, fslots, halo_k, halo_v, chead, cnext,
    part, xch, rsl, gat, sib,
    in_sem, out_sem, bs_send, bs_recv, fs_send, fs_recv, hf_send, hf_recv, hb_send, hb_recv,
    x_send, x_recv, r_send, r_recv, g_send, g_recv, s_send, s_recv,
):
    length, channels = q1.shape
    ntaps = taps.shape[0]
    modes = res.shape[0]
    groups = channels // (2 * WIDE)
    chips = size // 2
    slots, share = part.shape[2], part.shape[2] // chips
    lanes = WIDE // 128
    me = lax.axis_index("ctx")
    core, chip = lax.rem(me, 2), me // 2
    peer = me + 1 - 2 * core

    barrier = pltpu.get_barrier_semaphore()
    for k in range(1, size):
        pl.semaphore_signal(
            barrier, inc=1, device_id={"ctx": lax.rem(me + k, size)},
            device_id_type=pl.DeviceIdType.MESH,
        )

    loads = []
    for n, (src, dst) in enumerate(
        [
            (q2_in, q2), (co_in, co), (th_in, thr.at[pl.ds(0, 2 * ntaps)]), (th_in, thf.at[pl.ds(0, 2 * ntaps)]),
            (tn_in, tn), (res_in, res), (taps_in, taps), (tf_in, tf), (ti_in, ti),
            (k1_in, k1), (v1_in, v1), (q1_in, q1), (k2_in, k2),
        ]
    ):
        copy = pltpu.make_async_copy(src, dst, in_sem.at[n])
        copy.start()
        loads.append(copy)

    def remote(src, dst, send, recv, target):
        return pltpu.make_async_remote_copy(
            src_ref=src, dst_ref=dst, send_sem=send, recv_sem=recv,
            device_id={"ctx": target}, device_id_type=pl.DeviceIdType.MESH,
        )

    def cols(t):
        return pl.ds(pl.multiple_of(t * WIDE, WIDE), WIDE)

    def wide_cols(g):
        return pl.ds(pl.multiple_of(g * 2 * WIDE, 2 * WIDE), 2 * WIDE)

    def rate_at(shape, dim):
        at = lax.rem(lax.broadcasted_iota(jnp.int32, shape, dim), modes)
        out = jnp.zeros(shape, f32)
        for m in range(modes):
            out = jnp.where(at == m, rates[m], out)
        return out

    def scale_of(rate):
        x = 2.0 * rate
        tail = 1.0 - x * (1.0 / 8.0)
        for n in range(7, 1, -1):
            tail = 1.0 - x * (1.0 / n) * tail
        return jnp.sqrt(x * tail)

    def iota(shape, dim):
        return lax.broadcasted_iota(jnp.int32, shape, dim)

    def first_rows(x):
        return jnp.where(iota(x.shape, 0) < modes, x, 0.0)

    def lane_parts(x):
        hi = x.astype(bf16).astype(f32)
        at = iota(x.shape, 1) // modes
        return jnp.where(at < 2, hi, jnp.where(at == 2, x - hi, 0.0)).astype(bf16)

    rows_long = rate_at((2 * modes, length), 0)
    places = iota((2 * modes, length), 1).astype(f32)
    rise_t[...] = three_lanes(first_rows(jnp.exp(-rows_long * places)))

    @pl.when(me == 0)
    def _():
        halo_k[...] = jnp.zeros_like(halo_k)
        halo_v[...] = jnp.zeros_like(halo_v)

    @pl.when(me == size - 1)
    def _():
        cnext[...] = jnp.zeros_like(cnext)

    for k in range(1, size):
        @pl.when(me + k >= size)
        def _():
            bslots[k - 1] = jnp.zeros_like(bstate)

        @pl.when(me - k < 0)
        def _():
            fslots[:, k - 1] = jnp.zeros((groups, modes, 2 * WIDE), f32)

    if part.shape[2] > (ntaps + modes) // 8 * lanes:
        used = (ntaps + modes) // 8 * lanes
        part[:, :, used:] = jnp.zeros((groups, 2, slots - used, 8, 128), f32)

    loads[0].wait()
    loads[1].wait()

    def first(t, carry):
        at = cols(t)
        cotan = co[:, at].astype(f32) * q2[:, at].astype(f32)
        bstate[:, at] = dot(rise_t[...], three(cotan))[:modes]
        return carry

    lax.fori_loop(0, 2 * groups, first, 0)
    pl.semaphore_wait(barrier, size - 1)

    def back_state(k, target):
        return remote(bstate, bslots.at[k - 1], bs_send.at[k - 1], bs_recv.at[k - 1], target)

    for k in range(1, size):
        @pl.when(me - k >= 0)
        def _():
            back_state(k, me - k).start()

    def halo_copies(g, target):
        rows = pl.ds(length - ntaps, ntaps)
        return (
            remote(k1_in.at[rows, wide_cols(g)], halo_k.at[g], hf_send.at[0, g], hf_recv.at[0, g], target),
            remote(v1_in.at[rows, wide_cols(g)], halo_v.at[g], hf_send.at[1, g], hf_recv.at[1, g], target),
        )

    @pl.when(me + 1 < size)
    def _():
        for g in range(groups):
            for copy in halo_copies(g, me + 1):
                copy.start()

    for copy in loads[2:]:
        copy.wait()

    rows_short = rate_at((2 * modes, ntaps), 0)
    places = iota((2 * modes, ntaps), 1).astype(f32)
    thr[2 * ntaps :] = three_lanes(first_rows(jnp.exp(-rows_short * places)))
    thf[2 * ntaps :] = three_lanes(first_rows(jnp.exp(-rows_short * (ntaps - 1.0 - places))))
    scaled = first_rows(scale_of(rows_short) * jnp.exp(-rows_short * places))
    back_table = jnp.concatenate(
        [tn[:, : 2 * ntaps], tn[:, 4 * ntaps :], tn[:, : 2 * ntaps]], 0
    )
    unit = 1.0 / ntaps
    mst_t[...] = three_lanes((unit * factor) * dot(three_lanes(scaled), back_table))
    lane_rate = rate_at((ntaps, 4 * modes), 1)
    places = iota((ntaps, 4 * modes), 0).astype(f32)
    lane_scale = scale_of(lane_rate)
    spread = dot(thr[: 2 * ntaps], three(lane_scale * jnp.exp(-lane_rate * places)))
    ms_t[...] = lane_parts(unit * spread)
    tail_t[...] = lane_parts(lane_scale * jnp.exp(-lane_rate * (ntaps - places)))
    lane_rate = rate_at((length, 4 * modes), 1)
    places = iota((length, 4 * modes), 0).astype(f32)
    lead_t[...] = lane_parts(scale_of(lane_rate) * jnp.exp(-lane_rate * (places + 1.0)))
    mode_rate = rate_at((modes, WIDE), 0)
    over_block = jnp.exp(-mode_rate * float(ntaps))
    over_device = jnp.exp(-mode_rate * float(length))
    one_step = (factor * scale_of(mode_rate)) * jnp.exp(-mode_rate)
    nblocks = length // ntaps
    spec = 2 * ntaps

    def second(t, carry):
        at = cols(t)
        cotan = co[:, at].astype(f32) * q2[:, at].astype(f32)
        fs = dot(ms_t[...], three_small(res[:, at]))
        fspec[:, at] = fs
        for b in range(nblocks):
            rows = slice(b * ntaps, (b + 1) * ntaps)
            both = dot(thr[...], three(cotan[rows]))
            ls = both[:spec]
            lspec[b, :, at] = ls
            kback[b, :, at] = both[spec : spec + modes]
            lback[rows, at] = dot(tn[...], three(cmul_conj(fs, ls)))
        ts = dot(thr[:spec], three(taps[:, at] * unit))
        tspec[:, at] = ts
        mixed = k1[:, at].astype(f32) * v1[:, at].astype(f32)
        w = dot(tf[...], three(mixed))
        wone[:, at] = w
        mr_one[:, at] = dot(ti[...], three(cmul(ts, w)))
        return carry

    lax.fori_loop(0, 2 * groups, second, 0)

    for k in range(1, size):
        @pl.when(me + k < size)
        def _():
            back_state(k, me + k).wait_recv()

    def cot_copy(t, target):
        return remote(chead.at[t], cnext.at[t], hb_send.at[t], hb_recv.at[t], target)

    def front_copy(g, k, target):
        return remote(fstate.at[g], fslots.at[g, k - 1], fs_send.at[g, k - 1], fs_recv.at[g, k - 1], target)

    def third(p, g):
        t = 2 * g + p
        at = cols(t)
        inner = pl.ds(pl.multiple_of(p * WIDE, WIDE), WIDE)
        r = res[:, at]
        ts, fs = tspec[:, at], fspec[:, at]
        state = bslots[size - 2, :, at]
        for k in range(size - 2, 0, -1):
            state = over_device * state + bslots[k - 1, :, at]
        later = [over_block * state + kback[1, :, at], state]
        cotan = co[:, at].astype(f32)
        key_li, query = k2[:, at].astype(f32), q1[:, at].astype(f32)
        back = lback[:, at] + jnp.concatenate(
            [dot(tail_t[...], three_small(r * later[b])) for b in range(nblocks)], 0
        )
        mr_grad = cotan + key_li * back
        grad = mr_grad * query
        hi, lo = split(grad)
        chead[t, 0] = hi[:ntaps]
        chead[t, 1] = lo[:ntaps]

        @pl.when(me > 0)
        def _():
            cot_copy(t, me - 1).start()

        cs = []
        for b in range(nblocks):
            rows = slice(b * ntaps, (b + 1) * ntaps)
            cs.append(dot(thr[:spec], jnp.concatenate([hi[rows], lo[rows], hi[rows]], 0)))
        ctail[:, at] = cs[1]

        prior = halo_k[g, :, inner].astype(f32) * halo_v[g, :, inner].astype(f32)
        mixed = k1[:ntaps, at].astype(f32) * v1[:ntaps, at].astype(f32)
        w0 = dot(tf[...], three(jnp.concatenate([prior, mixed], 0)))
        w1 = wone[:, at]
        mr0 = dot(ti[...], three(cmul(ts, w0)))
        mr = jnp.concatenate([mr0, mr_one[:, at]], 0)
        gq1[:, at] = (mr_grad * mr).astype(bf16)
        mr_out = query * mr
        gk2[:, at] = (mr_out * back).astype(bf16)
        x = key_li * mr_out
        taps_part = dot(tn[...], three(conj_turned(w0, cs[0]) + conj_turned(w1, cs[1])))
        taps_part = taps_part * (unit * factor)
        for i in range(ntaps // 8):
            for j in range(lanes):
                part[g, p, i * lanes + j] = taps_part[8 * i : 8 * i + 8, 128 * j : 128 * j + 128]

        lag, fronts, near = None, [], []
        for b in range(nblocks):
            rows = slice(b * ntaps, (b + 1) * ntaps)
            both = dot(thf[...], three(x[rows]))
            xs = both[:spec]
            fronts.append(both[spec : spec + modes])
            now = cmul_conj(xs, lspec[b, :, at])
            lag = now if lag is None else lag + now
            near.append(dot(tn[...], three(cmul(fs, xs))))
        near[1] = near[1] + dot(lead_t[:ntaps], three_small(r * fronts[0]))
        lconv[:, at] = jnp.concatenate(near, 0)
        fstate[g, :, inner] = over_block * fronts[0] + fronts[1]
        res_part = dot(mst_t[...], three(lag))[:modes]
        res_part = res_part + one_step * (fronts[0] * later[0] + fronts[1] * later[1])
        for j in range(lanes):
            part[g, p, ntaps // 8 * lanes + j] = res_part[:, 128 * j : 128 * j + 128]

        mg = dot(tn[...], three(cmul_conj(ts, add_turned(cs[0], cs[1]))))
        gk1[:ntaps, at] = (mg * v1[:ntaps, at].astype(f32)).astype(bf16)
        gv1[:ntaps, at] = (mg * k1[:ntaps, at].astype(f32)).astype(bf16)
        return g

    def fourth(p, g):
        t = 2 * g + p
        at = cols(t)
        inner = pl.ds(pl.multiple_of(p * WIDE, WIDE), WIDE)
        state = fslots[g, size - 2, :, inner]
        for k in range(size - 2, 0, -1):
            state = over_device * state + fslots[g, k - 1, :, inner]
        conv = lconv[:, at] + dot(lead_t[...], three_small(res[:, at] * state))
        gq2[:, at] = (co[:, at].astype(f32) * conv).astype(bf16)
        hi, lo = cnext[t, 0], cnext[t, 1]
        nxt = dot(thr[:spec], jnp.concatenate([hi, lo, hi], 0))
        mg = dot(tn[...], three(cmul_conj(tspec[:, at], add_turned(ctail[:, at], nxt))))
        gk1[ntaps:, at] = (mg * v1[ntaps:, at].astype(f32)).astype(bf16)
        gv1[ntaps:, at] = (mg * k1[ntaps:, at].astype(f32)).astype(bf16)
        return g

    def to_peer(g):
        return remote(part.at[g, 1 - core], xch.at[g], x_send.at[g], x_recv.at[g], peer)

    def scatter(g, j, other):
        return remote(
            part.at[g, core, pl.ds(other * share, share)], rsl.at[g, j - 1],
            r_send.at[g, j - 1], r_recv.at[g, j - 1], 2 * other + core,
        )

    def gather(g, j, other, owner):
        mine = pl.ds(owner * share, share)
        return remote(
            gat.at[g, mine], gat.at[g, mine], g_send.at[g, j - 1], g_recv.at[g, j - 1], 2 * other + core
        )

    def to_sib(g):
        return remote(gat.at[g], sib.at[g], s_send.at[g], s_recv.at[g], peer)

    def after(j):
        return lax.rem(chip + j, chips)

    def before(j):
        return lax.rem(chip + chips - j, chips)

    def stage_two(g):
        to_peer(g).wait_recv()
        part[g, core] = part[g, core] + xch[g]
        for j in range(1, chips):
            scatter(g, j, after(j)).start()

    def stage_three(g):
        mine = pl.ds(chip * share, share)
        total = part[g, core, mine]
        for j in range(1, chips):
            scatter(g, j, before(j)).wait_recv()
            total = total + rsl[g, j - 1]
        gat[g, mine] = total
        for j in range(1, chips):
            gather(g, j, after(j), chip).start()

    def stage_four(g):
        for j in range(1, chips):
            gather(g, j, before(j), before(j)).wait_recv()
        to_sib(g).start()

    def out_copy(n, g):
        src, dst = (
            (gq1, gq1_out), (gk2, gk2_out), (gk1, gk1_out), (gv1, gv1_out), (gq2, gq2_out),
            (taps_st, taps_out), (res_st, res_out),
        )[n]
        at = wide_cols(g)
        return pltpu.make_async_copy(src.at[:, at], dst.at[:, at], out_sem.at[n, g])

    def stage_five(g):
        to_sib(g).wait_recv()
        for src, half in ((gat, core), (sib, 1 - core)):
            for j in range(lanes):
                at = pl.ds(pl.multiple_of((2 * g + half) * WIDE + 128 * j, 128), 128)
                for i in range(ntaps // 8):
                    taps_st[8 * i : 8 * i + 8, at] = src[g, i * lanes + j]
                res_st[:, at] = src[g, ntaps // 8 * lanes + j]
        out_copy(5, g).start()
        out_copy(6, g).start()

    def stages(s):
        for n, stage in enumerate((stage_two, stage_three, stage_four, stage_five)):
            g = s - (n + 1)

            @pl.when((g >= 0) & (g < groups))
            def _():
                stage(g)

    def third_group(g, carry):
        @pl.when(me > 0)
        def _():
            for copy in halo_copies(g, me - 1):
                copy.wait_recv()

        lax.fori_loop(0, 2, third, g)
        to_peer(g).start()
        for k in range(1, size):
            @pl.when(me + k < size)
            def _():
                front_copy(g, k, me + k).start()

        out_copy(0, g).start()
        out_copy(1, g).start()
        stages(g)
        return carry

    lax.fori_loop(0, groups, third_group, 0)

    def fourth_group(s, carry):
        g = s - groups

        @pl.when(g < groups)
        def _():
            for k in range(1, size):
                @pl.when(me - k >= 0)
                def _():
                    front_copy(g, k, me - k).wait_recv()

            @pl.when(me + 1 < size)
            def _():
                cot_copy(2 * g, me + 1).wait_recv()
                cot_copy(2 * g + 1, me + 1).wait_recv()

            lax.fori_loop(0, 2, fourth, g)
            for n in (2, 3, 4):
                out_copy(n, g).start()

        stages(s)
        return carry

    lax.fori_loop(groups, groups + max(groups, 4), fourth_group, 0)

    for k in range(1, size):
        @pl.when(me - k >= 0)
        def _():
            back_state(k, me - k).wait_send()

    def finish(g, carry):
        @pl.when(me + 1 < size)
        def _():
            for copy in halo_copies(g, me + 1):
                copy.wait_send()

        @pl.when(me > 0)
        def _():
            cot_copy(2 * g, me - 1).wait_send()
            cot_copy(2 * g + 1, me - 1).wait_send()

        for k in range(1, size):
            @pl.when(me + k < size)
            def _():
                front_copy(g, k, me + k).wait_send()

        to_peer(g).wait_send()
        to_sib(g).wait_send()
        for j in range(1, chips):
            scatter(g, j, after(j)).wait_send()
            gather(g, j, after(j), chip).wait_send()
        for n in range(7):
            out_copy(n, g).wait()
        return carry

    lax.fori_loop(0, groups, finish, 0)


def per_device(q1, k1, v1, q2, k2, co, mr_taps, decay_rates, residues):
    size = lax.axis_size("ctx")
    length, channels = q1.shape
    ntaps, modes = mr_taps.shape[0], residues.shape[0]
    groups, chips = channels // (2 * WIDE), size // 2
    nblocks, spec = length // ntaps, 2 * ntaps
    used = (ntaps + modes) // 8 * (WIDE // 128)
    share = -(-used // chips)
    slots = share * chips
    factor = 1.0 / math.sqrt(length * size)
    consts = [jnp.asarray(t) for t in tables(ntaps)]

    def vm(*shape, dtype=f32):
        return pltpu.VMEM(shape, dtype)

    dma = lambda *shape: pltpu.SemaphoreType.DMA(shape)
    wide = lambda: vm(length, channels, dtype=bf16)
    scratch = [
        wide(), wide(), wide(), wide(), wide(), wide(),
        vm(ntaps, channels), vm(modes, channels),
        vm(spec, 3 * spec, dtype=bf16), vm(spec + 2 * modes, 3 * ntaps, dtype=bf16),
        vm(spec + 2 * modes, 3 * ntaps, dtype=bf16),
        vm(ntaps, 3 * spec, dtype=bf16), vm(ntaps, 3 * spec, dtype=bf16),
        vm(2 * modes, 3 * length, dtype=bf16), vm(spec, 4 * modes, dtype=bf16),
        vm(2 * modes, 3 * spec, dtype=bf16), vm(length, 4 * modes, dtype=bf16),
        vm(ntaps, 4 * modes, dtype=bf16),
        vm(nblocks, spec, channels), vm(nblocks, modes, channels), vm(spec, channels), vm(spec, channels),
        vm(spec, channels), vm(ntaps, channels), vm(length, channels), vm(length, channels),
        vm(spec, channels),
        wide(), wide(), wide(), wide(), wide(), vm(ntaps, channels), vm(modes, channels),
        vm(modes, channels), vm(size - 1, modes, channels),
        vm(groups, modes, 2 * WIDE), vm(groups, size - 1, modes, 2 * WIDE),
        vm(groups, ntaps, 2 * WIDE, dtype=bf16), vm(groups, ntaps, 2 * WIDE, dtype=bf16),
        vm(2 * groups, 2, ntaps, WIDE, dtype=bf16), vm(2 * groups, 2, ntaps, WIDE, dtype=bf16),
        vm(groups, 2, slots, 8, 128), vm(groups, slots, 8, 128), vm(groups, chips - 1, share, 8, 128),
        vm(groups, slots, 8, 128), vm(groups, slots, 8, 128),
        dma(13), dma(7, groups), dma(size - 1), dma(size - 1), dma(groups, size - 1), dma(groups, size - 1),
        dma(2, groups), dma(2, groups), dma(2 * groups), dma(2 * groups),
        dma(groups), dma(groups), dma(groups, chips - 1), dma(groups, chips - 1),
        dma(groups, chips - 1), dma(groups, chips - 1), dma(groups), dma(groups),
    ]
    out = jax.ShapeDtypeStruct((length, channels), bf16)
    anywhere = pl.BlockSpec(memory_space=pl.ANY)
    specs = [anywhere] * 7 + [pl.BlockSpec(memory_space=pltpu.SMEM)] + [anywhere] * 5
    return pl.pallas_call(
        lambda *refs: kernel(size, factor, *refs),
        out_shape=(out,) * 5
        + (
            jax.ShapeDtypeStruct((ntaps, channels), f32),
            jax.ShapeDtypeStruct((modes, channels), f32),
        ),
        in_specs=specs,
        out_specs=(anywhere,) * 7,
        scratch_shapes=scratch,
        compiler_params=pltpu.CompilerParams(
            collective_id=0, has_side_effects=True, vmem_limit_bytes=60 * 2**20
        ),
        name="backward",
    )(q1, k1, v1, q2, k2, co, mr_taps, decay_rates, residues, *consts)


def solution(mesh):
    whole, cols = P("ctx", "tp"), P(None, "tp")
    return jax.shard_map(
        per_device,
        mesh=mesh,
        in_specs=(whole,) * 6 + (cols, P(), cols),
        out_specs=(whole,) * 5 + (cols, cols),
        check_vma=False,
    )
```

```python
import math

import numpy as np
import ml_dtypes
import jax
import jax.numpy as jnp
from jax import lax
from jax.experimental import pallas as pl
from jax.experimental.pallas import tpu as pltpu
from jax.sharding import PartitionSpec as P

f32, bf16 = jnp.float32, jnp.bfloat16
WIDE = 256


def tables(taps):
    size, half = 2 * taps, taps // 2
    order = np.concatenate([np.arange(0, taps, 2), np.arange(1, taps, 2)])
    angle = (2.0 * np.pi / size) * (order[:, None] + 0.5) * np.arange(size)[None, :]
    full = np.concatenate([np.cos(angle), -np.sin(angle)], 0)

    def three(table):
        hi = table.astype(ml_dtypes.bfloat16)
        lo = (table - hi.astype(np.float64)).astype(ml_dtypes.bfloat16)
        return np.concatenate([hi, hi, lo], 1)

    return (
        three(full),
        three(full[:, :taps]),
        three(full[:, :taps].T),
        three(full[:, taps:].T),
    )


def split(x):
    hi = x.astype(bf16)
    return hi, (x - hi.astype(f32)).astype(bf16)


def three(x):
    hi, lo = split(x)
    return jnp.concatenate([hi, lo, hi], 0)


def three_small(x):
    hi = x.astype(bf16).astype(f32)
    return jnp.concatenate([hi, x - hi, hi, jnp.zeros_like(x)], 0).astype(bf16)


def three_lanes(x):
    hi, lo = split(x)
    return jnp.concatenate([hi, hi, lo], 1)


def dot(a, b):
    return jnp.dot(a, b, preferred_element_type=f32)


def parts_of(z):
    n = z.shape[0] // 2
    return z[:n], z[n:]


def cmul(a, b):
    (ar, ai), (br, bi) = parts_of(a), parts_of(b)
    return jnp.concatenate([ar * br - ai * bi, ar * bi + ai * br], 0)


def cmul_conj(a, b):
    (ar, ai), (br, bi) = parts_of(a), parts_of(b)
    return jnp.concatenate([ar * br + ai * bi, ar * bi - ai * br], 0)


def turned(z):
    q = z.shape[0] // 4
    return jnp.concatenate([z[2 * q : 3 * q], -z[3 * q :], -z[:q], z[q : 2 * q]], 0)


def add_turned(y, z):
    q = z.shape[0] // 4
    return jnp.concatenate(
        [
            y[:q] + z[2 * q : 3 * q],
            y[q : 2 * q] - z[3 * q :],
            y[2 * q : 3 * q] - z[:q],
            y[3 * q :] + z[q : 2 * q],
        ],
        0,
    )


def conj_turned(w, z):
    n = w.shape[0] // 2
    h = n // 2
    wr, wi, zr, zi = w[:n], w[n:], z[:n], z[n:]
    re = wr * zi - wi * zr
    im = wr * zr + wi * zi
    return jnp.concatenate([re[:h], -re[h:], -im[:h], im[h:]], 0)


def kernel(
    size, factor,
    q1_in, k1_in, v1_in, q2_in, k2_in, co_in, taps_in, rates, res_in, tf_in, th_in, tn_in, ti_in,
    gq1, gk1, gv1, gq2, gk2, taps_st, res_st,
    q1, k1, v1, q2, k2, co, taps, res, tf, thr, thf, tn, ti,
    rise_t, ms_t, mst_t, lead_t, tail_t,
    lspec, kback, tspec, fspec, wone, mr_one, lback, lconv, ctail,
    bstate, bslots, fstate, fslots, halo_k, halo_v, chead, cnext,
    part, xch, rsl, gat, sib,
    in_sem, bs_send, bs_recv, fs_send, fs_recv, hf_send, hf_recv, hb_send, hb_recv,
    x_send, x_recv, r_send, r_recv, g_send, g_recv, s_send, s_recv,
):
    length, channels = q1.shape
    ntaps = taps.shape[0]
    modes = res.shape[0]
    groups = channels // (2 * WIDE)
    chips = size // 2
    slots, share = part.shape[2], part.shape[2] // chips
    lanes = WIDE // 128
    me = lax.axis_index("ctx")
    core, chip = lax.rem(me, 2), me // 2
    peer = me + 1 - 2 * core

    barrier = pltpu.get_barrier_semaphore()
    for k in range(1, size):
        pl.semaphore_signal(
            barrier, inc=1, device_id={"ctx": lax.rem(me + k, size)},
            device_id_type=pl.DeviceIdType.MESH,
        )

    loads = []
    for n, (src, dst) in enumerate(
        [
            (q2_in, q2), (co_in, co), (th_in, thr.at[pl.ds(0, 2 * ntaps)]), (th_in, thf.at[pl.ds(0, 2 * ntaps)]),
            (tn_in, tn), (res_in, res), (taps_in, taps), (tf_in, tf), (ti_in, ti),
            (k1_in, k1), (v1_in, v1), (q1_in, q1), (k2_in, k2),
        ]
    ):
        copy = pltpu.make_async_copy(src, dst, in_sem.at[n])
        copy.start()
        loads.append(copy)

    def remote(src, dst, send, recv, target):
        return pltpu.make_async_remote_copy(
            src_ref=src, dst_ref=dst, send_sem=send, recv_sem=recv,
            device_id={"ctx": target}, device_id_type=pl.DeviceIdType.MESH,
        )

    def wide_cols(g):
        return pl.ds(pl.multiple_of(g * 2 * WIDE, 2 * WIDE), 2 * WIDE)

    def rate_at(shape, dim):
        at = lax.rem(lax.broadcasted_iota(jnp.int32, shape, dim), modes)
        out = jnp.zeros(shape, f32)
        for m in range(modes):
            out = jnp.where(at == m, rates[m], out)
        return out

    def scale_of(rate):
        x = 2.0 * rate
        tail = 1.0 - x * (1.0 / 8.0)
        for n in range(7, 1, -1):
            tail = 1.0 - x * (1.0 / n) * tail
        return jnp.sqrt(x * tail)

    def iota(shape, dim):
        return lax.broadcasted_iota(jnp.int32, shape, dim)

    def first_rows(x):
        return jnp.where(iota(x.shape, 0) < modes, x, 0.0)

    def lane_parts(x):
        hi = x.astype(bf16).astype(f32)
        at = iota(x.shape, 1) // modes
        return jnp.where(at < 2, hi, jnp.where(at == 2, x - hi, 0.0)).astype(bf16)

    rows_long = rate_at((2 * modes, length), 0)
    places = iota((2 * modes, length), 1).astype(f32)
    rise_t[...] = three_lanes(first_rows(jnp.exp(-rows_long * places)))

    @pl.when(me == 0)
    def _():
        halo_k[...] = jnp.zeros_like(halo_k)
        halo_v[...] = jnp.zeros_like(halo_v)

    @pl.when(me == size - 1)
    def _():
        cnext[...] = jnp.zeros_like(cnext)

    for k in range(1, size):
        @pl.when(me + k >= size)
        def _():
            bslots[k - 1] = jnp.zeros_like(bstate)

        @pl.when(me - k < 0)
        def _():
            fslots[:, k - 1] = jnp.zeros((groups, modes, 2 * WIDE), f32)

    if part.shape[2] > (ntaps + modes) // 8 * lanes:
        used = (ntaps + modes) // 8 * lanes
        part[:, :, used:] = jnp.zeros((groups, 2, slots - used, 8, 128), f32)

    loads[0].wait()
    loads[1].wait()

    def first(g, carry):
        at = wide_cols(g)
        cotan = co[:, at].astype(f32) * q2[:, at].astype(f32)
        bstate[:, at] = dot(rise_t[...], three(cotan))[:modes]
        return carry

    lax.fori_loop(0, groups, first, 0)
    pl.semaphore_wait(barrier, size - 1)

    def back_state(k, target):
        return remote(bstate, bslots.at[k - 1], bs_send.at[k - 1], bs_recv.at[k - 1], target)

    for k in range(1, size):
        @pl.when(me - k >= 0)
        def _():
            back_state(k, me - k).start()

    def halo_copies(g, target):
        rows = pl.ds(length - ntaps, ntaps)
        return (
            remote(k1_in.at[rows, wide_cols(g)], halo_k.at[g], hf_send.at[0, g], hf_recv.at[0, g], target),
            remote(v1_in.at[rows, wide_cols(g)], halo_v.at[g], hf_send.at[1, g], hf_recv.at[1, g], target),
        )

    @pl.when(me + 1 < size)
    def _():
        for g in range(groups):
            for copy in halo_copies(g, me + 1):
                copy.start()

    for copy in loads[2:5]:
        copy.wait()

    rows_short = rate_at((2 * modes, ntaps), 0)
    places = iota((2 * modes, ntaps), 1).astype(f32)
    thr[2 * ntaps :] = three_lanes(first_rows(jnp.exp(-rows_short * places)))
    thf[2 * ntaps :] = three_lanes(first_rows(jnp.exp(-rows_short * (ntaps - 1.0 - places))))
    scaled = first_rows(scale_of(rows_short) * jnp.exp(-rows_short * places))
    back_table = jnp.concatenate(
        [tn[:, : 2 * ntaps], tn[:, 4 * ntaps :], tn[:, : 2 * ntaps]], 0
    )
    unit = 1.0 / ntaps
    mst_t[...] = three_lanes((unit * factor) * dot(three_lanes(scaled), back_table))
    lane_rate = rate_at((ntaps, 4 * modes), 1)
    places = iota((ntaps, 4 * modes), 0).astype(f32)
    lane_scale = scale_of(lane_rate)
    spread = dot(thr[: 2 * ntaps], three(lane_scale * jnp.exp(-lane_rate * places)))
    ms_t[...] = lane_parts(unit * spread)
    tail_t[...] = lane_parts(lane_scale * jnp.exp(-lane_rate * (ntaps - places)))
    lane_rate = rate_at((length, 4 * modes), 1)
    places = iota((length, 4 * modes), 0).astype(f32)
    lead_t[...] = lane_parts(scale_of(lane_rate) * jnp.exp(-lane_rate * (places + 1.0)))
    mode_rate = rate_at((modes, 2 * WIDE), 0)
    over_block = jnp.exp(-mode_rate * float(ntaps))
    over_device = jnp.exp(-mode_rate * float(length))
    one_step = (factor * scale_of(mode_rate)) * jnp.exp(-mode_rate)
    nblocks = length // ntaps
    spec = 2 * ntaps

    blocks = [slice(b * ntaps, (b + 1) * ntaps) for b in range(nblocks)]
    across = 2 * WIDE

    def beside(arrays):
        return jnp.concatenate(arrays, 1)

    def apart(array):
        return [array[:, i : i + across] for i in range(0, array.shape[1], across)]

    def second(g, carry):
        at = wide_cols(g)
        cotan = co[:, at].astype(f32) * q2[:, at].astype(f32)
        mixed = k1[:, at].astype(f32) * v1[:, at].astype(f32)
        w = dot(tf[...], three(mixed))
        wone[:, at] = w
        fs = dot(ms_t[...], three_small(res[:, at]))
        fspec[:, at] = fs
        both = apart(dot(thr[...], beside([three(cotan[rows]) for rows in blocks] + [three(taps[:, at] * unit)])))
        ts = both[nblocks][:spec]
        tspec[:, at] = ts
        for b in range(nblocks):
            lspec[b, :, at] = both[b][:spec]
            kback[b, :, at] = both[b][spec : spec + modes]
        mr_one[:, at] = dot(ti[...], three(cmul(ts, w)))
        near = apart(dot(tn[...], beside([three(cmul_conj(fs, both[b][:spec])) for b in range(nblocks)])))
        for b in range(nblocks):
            lback[blocks[b], at] = near[b]
        return carry

    for copy in loads[5:]:
        copy.wait()

    lax.fori_loop(0, groups, second, 0)

    for k in range(1, size):
        @pl.when(me + k < size)
        def _():
            back_state(k, me + k).wait_recv()

    def cot_copy(g, target):
        return remote(chead.at[g], cnext.at[g], hb_send.at[g], hb_recv.at[g], target)

    def front_copy(g, k, target):
        return remote(fstate.at[g], fslots.at[g, k - 1], fs_send.at[g, k - 1], fs_recv.at[g, k - 1], target)

    def third(g):
        at = wide_cols(g)
        r = res[:, at]
        ts, fs = tspec[:, at], fspec[:, at]
        cotan = co[:, at].astype(f32)
        key_li, query = k2[:, at].astype(f32), q1[:, at].astype(f32)
        state = bslots[size - 2, :, at]
        for k in range(size - 2, 0, -1):
            state = over_device * state + bslots[k - 1, :, at]
        later = [over_block * state + kback[1, :, at], state]
        far = apart(dot(tail_t[...], beside([three_small(r * later[b]) for b in range(nblocks)])))
        prior = halo_k[g].astype(f32) * halo_v[g].astype(f32)
        mixed = k1[:ntaps, at].astype(f32) * v1[:ntaps, at].astype(f32)
        w0 = dot(tf[...], three(jnp.concatenate([prior, mixed], 0)))
        back = lback[:, at] + jnp.concatenate(far, 0)
        mr_grad = cotan + key_li * back
        grad = mr_grad * query
        hi, lo = split(grad)
        chead[g, 0] = hi[:ntaps]
        chead[g, 1] = lo[:ntaps]

        @pl.when(me > 0)
        def _():
            cot_copy(g, me - 1).start()

        mr0 = dot(ti[...], three(cmul(ts, w0)))
        cs = apart(dot(thr[:spec], beside([jnp.concatenate([hi[rows], lo[rows], hi[rows]], 0) for rows in blocks])))
        ctail[:, at] = cs[1]
        w1 = wone[:, at]
        mr = jnp.concatenate([mr0, mr_one[:, at]], 0)
        gq1[:, at] = (mr_grad * mr).astype(bf16)
        mr_out = query * mr
        gk2[:, at] = (mr_out * back).astype(bf16)
        x = key_li * mr_out
        both = apart(dot(thf[...], beside([three(x[rows]) for rows in blocks])))
        turn = conj_turned(w0, cs[0]) + conj_turned(w1, cs[1])
        taps_part, mg = apart(dot(tn[...], beside([three(turn), three(cmul_conj(ts, add_turned(cs[0], cs[1])))])))
        taps_part = taps_part * (unit * factor)
        for p in range(2):
            for i in range(ntaps // 8):
                for j in range(lanes):
                    lane = p * WIDE + 128 * j
                    part[g, p, i * lanes + j] = taps_part[8 * i : 8 * i + 8, lane : lane + 128]
        gk1[:ntaps, at] = (mg * v1[:ntaps, at].astype(f32)).astype(bf16)
        gv1[:ntaps, at] = (mg * k1[:ntaps, at].astype(f32)).astype(bf16)

        fronts = [both[b][spec : spec + modes] for b in range(nblocks)]
        fstate[g] = over_block * fronts[0] + fronts[1]
        lag = cmul_conj(both[0][:spec], lspec[0, :, at]) + cmul_conj(both[1][:spec], lspec[1, :, at])
        near = apart(dot(tn[...], beside([three(cmul(fs, both[b][:spec])) for b in range(nblocks)])))
        near[1] = near[1] + dot(lead_t[:ntaps], three_small(r * fronts[0]))
        for b in range(nblocks):
            lconv[blocks[b], at] = near[b]
        res_part = dot(mst_t[...], three(lag))[:modes]
        res_part = res_part + one_step * (fronts[0] * later[0] + fronts[1] * later[1])
        for p in range(2):
            for j in range(lanes):
                lane = p * WIDE + 128 * j
                part[g, p, ntaps // 8 * lanes + j] = res_part[:, lane : lane + 128]

    def fourth(g):
        at = wide_cols(g)
        state = fslots[g, size - 2]
        for k in range(size - 2, 0, -1):
            state = over_device * state + fslots[g, k - 1]
        hi, lo = cnext[g, 0], cnext[g, 1]
        nxt = dot(thr[:spec], jnp.concatenate([hi, lo, hi], 0))
        conv = lconv[:, at] + dot(lead_t[...], three_small(res[:, at] * state))
        gq2[:, at] = (co[:, at].astype(f32) * conv).astype(bf16)
        mg = dot(tn[...], three(cmul_conj(tspec[:, at], add_turned(ctail[:, at], nxt))))
        gk1[ntaps:, at] = (mg * v1[ntaps:, at].astype(f32)).astype(bf16)
        gv1[ntaps:, at] = (mg * k1[ntaps:, at].astype(f32)).astype(bf16)

    def to_peer(g):
        return remote(part.at[g, 1 - core], xch.at[g], x_send.at[g], x_recv.at[g], peer)

    def scatter(g, j, other):
        return remote(
            part.at[g, core, pl.ds(other * share, share)], rsl.at[g, j - 1],
            r_send.at[g, j - 1], r_recv.at[g, j - 1], 2 * other + core,
        )

    def gather(g, j, other, owner):
        mine = pl.ds(owner * share, share)
        return remote(
            gat.at[g, mine], gat.at[g, mine], g_send.at[g, j - 1], g_recv.at[g, j - 1], 2 * other + core
        )

    def to_sib(g):
        return remote(gat.at[g], sib.at[g], s_send.at[g], s_recv.at[g], peer)

    def after(j):
        return lax.rem(chip + j, chips)

    def before(j):
        return lax.rem(chip + chips - j, chips)

    def stage_two(g):
        to_peer(g).wait_recv()
        part[g, core] = part[g, core] + xch[g]
        for j in range(1, chips):
            scatter(g, j, after(j)).start()

    def stage_three(g):
        mine = pl.ds(chip * share, share)
        total = part[g, core, mine]
        for j in range(1, chips):
            scatter(g, j, before(j)).wait_recv()
            total = total + rsl[g, j - 1]
        gat[g, mine] = total
        for j in range(1, chips):
            gather(g, j, after(j), chip).start()

    def stage_four(g):
        for j in range(1, chips):
            gather(g, j, before(j), before(j)).wait_recv()
        to_sib(g).start()

    def stage_five(g):
        to_sib(g).wait_recv()
        for src, half in ((gat, core), (sib, 1 - core)):
            for j in range(lanes):
                at = pl.ds(pl.multiple_of((2 * g + half) * WIDE + 128 * j, 128), 128)
                for i in range(ntaps // 8):
                    taps_st[8 * i : 8 * i + 8, at] = src[g, i * lanes + j]
                res_st[:, at] = src[g, ntaps // 8 * lanes + j]

    def stages(s):
        for n, stage in enumerate((stage_two, stage_three, stage_four, stage_five)):
            g = s - (n + 1)

            @pl.when((g >= 0) & (g < groups))
            def _():
                stage(g)

    def third_group(g, carry):
        @pl.when(me > 0)
        def _():
            for copy in halo_copies(g, me - 1):
                copy.wait_recv()

        third(g)
        to_peer(g).start()
        for k in range(1, size):
            @pl.when(me + k < size)
            def _():
                front_copy(g, k, me + k).start()

        stages(g)
        return carry

    lax.fori_loop(0, groups, third_group, 0)

    def fourth_group(s, carry):
        g = s - groups

        @pl.when(g < groups)
        def _():
            for k in range(1, size):
                @pl.when(me - k >= 0)
                def _():
                    front_copy(g, k, me - k).wait_recv()

            @pl.when(me + 1 < size)
            def _():
                cot_copy(g, me + 1).wait_recv()

            fourth(g)

        stages(s)
        return carry

    lax.fori_loop(groups, groups + max(groups, 4), fourth_group, 0)

    for k in range(1, size):
        @pl.when(me - k >= 0)
        def _():
            back_state(k, me - k).wait_send()

    def finish(g, carry):
        @pl.when(me + 1 < size)
        def _():
            for copy in halo_copies(g, me + 1):
                copy.wait_send()

        @pl.when(me > 0)
        def _():
            cot_copy(g, me - 1).wait_send()

        for k in range(1, size):
            @pl.when(me + k < size)
            def _():
                front_copy(g, k, me + k).wait_send()

        to_peer(g).wait_send()
        to_sib(g).wait_send()
        for j in range(1, chips):
            scatter(g, j, after(j)).wait_send()
            gather(g, j, after(j), chip).wait_send()
        return carry

    lax.fori_loop(0, groups, finish, 0)


def write_out(*refs):
    copies = [pltpu.make_async_copy(refs[i], refs[7 + i], refs[14].at[i]) for i in range(7)]
    for copy in copies:
        copy.start()
    for copy in copies:
        copy.wait()


def per_device(q1, k1, v1, q2, k2, co, mr_taps, decay_rates, residues):
    size = lax.axis_size("ctx")
    length, channels = q1.shape
    ntaps, modes = mr_taps.shape[0], residues.shape[0]
    groups, chips = channels // (2 * WIDE), size // 2
    nblocks, spec = length // ntaps, 2 * ntaps
    used = (ntaps + modes) // 8 * (WIDE // 128)
    share = -(-used // chips)
    slots = share * chips
    factor = 1.0 / math.sqrt(length * size)
    consts = [jnp.asarray(t) for t in tables(ntaps)]

    def vm(*shape, dtype=f32):
        return pltpu.VMEM(shape, dtype)

    dma = lambda *shape: pltpu.SemaphoreType.DMA(shape)
    wide = lambda: vm(length, channels, dtype=bf16)
    scratch = [
        wide(), wide(), wide(), wide(), wide(), wide(),
        vm(ntaps, channels), vm(modes, channels),
        vm(spec, 3 * spec, dtype=bf16), vm(spec + 2 * modes, 3 * ntaps, dtype=bf16),
        vm(spec + 2 * modes, 3 * ntaps, dtype=bf16),
        vm(ntaps, 3 * spec, dtype=bf16), vm(ntaps, 3 * spec, dtype=bf16),
        vm(2 * modes, 3 * length, dtype=bf16), vm(spec, 4 * modes, dtype=bf16),
        vm(2 * modes, 3 * spec, dtype=bf16), vm(length, 4 * modes, dtype=bf16),
        vm(ntaps, 4 * modes, dtype=bf16),
        vm(nblocks, spec, channels), vm(nblocks, modes, channels), vm(spec, channels), vm(spec, channels),
        vm(spec, channels), vm(ntaps, channels), vm(length, channels), vm(length, channels),
        vm(spec, channels),
        vm(modes, channels), vm(size - 1, modes, channels),
        vm(groups, modes, 2 * WIDE), vm(groups, size - 1, modes, 2 * WIDE),
        vm(groups, ntaps, 2 * WIDE, dtype=bf16), vm(groups, ntaps, 2 * WIDE, dtype=bf16),
        vm(groups, 2, ntaps, 2 * WIDE, dtype=bf16), vm(groups, 2, ntaps, 2 * WIDE, dtype=bf16),
        vm(groups, 2, slots, 8, 128), vm(groups, slots, 8, 128), vm(groups, chips - 1, share, 8, 128),
        vm(groups, slots, 8, 128), vm(groups, slots, 8, 128),
        dma(13), dma(size - 1), dma(size - 1), dma(groups, size - 1), dma(groups, size - 1),
        dma(2, groups), dma(2, groups), dma(groups), dma(groups),
        dma(groups), dma(groups), dma(groups, chips - 1), dma(groups, chips - 1),
        dma(groups, chips - 1), dma(groups, chips - 1), dma(groups), dma(groups),
    ]
    anywhere = pl.BlockSpec(memory_space=pl.ANY)
    specs = [anywhere] * 7 + [pl.BlockSpec(memory_space=pltpu.SMEM)] + [anywhere] * 5
    results = [((length, channels), bf16)] * 5 + [((ntaps, channels), f32), ((modes, channels), f32)]
    held = pl.pallas_call(
        lambda *refs: kernel(size, factor, *refs),
        out_shape=tuple(pltpu.VMEM(*r) for r in results),
        in_specs=specs,
        out_specs=(pl.BlockSpec(memory_space=pltpu.VMEM),) * 7,
        scratch_shapes=scratch,
        compiler_params=pltpu.CompilerParams(
            collective_id=0, has_side_effects=True, vmem_limit_bytes=50 * 2**20
        ),
        name="backward",
    )(q1, k1, v1, q2, k2, co, mr_taps, decay_rates, residues, *consts)
    held = [pltpu.with_memory_space_constraint(x, pltpu.VMEM) for x in held]
    return pl.pallas_call(
        write_out,
        out_shape=tuple(jax.ShapeDtypeStruct(*r) for r in results),
        in_specs=(pl.BlockSpec(memory_space=pltpu.VMEM),) * 7,
        out_specs=(anywhere,) * 7,
        scratch_shapes=[dma(7)],
        compiler_params=pltpu.CompilerParams(vmem_limit_bytes=2**20),
        name="write_out",
    )(*held)


def solution(mesh):
    whole, cols = P("ctx", "tp"), P(None, "tp")
    return jax.shard_map(
        per_device,
        mesh=mesh,
        in_specs=(whole,) * 6 + (cols, P(), cols),
        out_specs=(whole,) * 5 + (cols, cols),
        check_vma=False,
    )
```

```python
import math

import numpy as np
import ml_dtypes
import jax
import jax.numpy as jnp
from jax import lax
from jax.experimental import pallas as pl
from jax.experimental.pallas import tpu as pltpu
from jax.sharding import PartitionSpec as P

f32, bf16 = jnp.float32, jnp.bfloat16
WIDE = 256


def tables(taps):
    size, half = 2 * taps, taps // 2
    order = np.concatenate([np.arange(0, taps, 2), np.arange(1, taps, 2)])
    angle = (2.0 * np.pi / size) * (order[:, None] + 0.5) * np.arange(size)[None, :]
    full = np.concatenate([np.cos(angle), -np.sin(angle)], 0)

    def three(table):
        hi = table.astype(ml_dtypes.bfloat16)
        lo = (table - hi.astype(np.float64)).astype(ml_dtypes.bfloat16)
        return np.concatenate([hi, hi, lo], 1)

    return (
        three(full),
        three(full[:, :taps]),
        three(full[:, :taps].T),
        three(full[:, taps:].T),
    )


def split(x):
    hi = x.astype(bf16)
    return hi, (x - hi.astype(f32)).astype(bf16)


def three(x):
    hi, lo = split(x)
    return jnp.concatenate([hi, lo, hi], 0)


def three_small(x):
    hi = x.astype(bf16).astype(f32)
    return jnp.concatenate([hi, x - hi, hi, jnp.zeros_like(x)], 0).astype(bf16)


def three_lanes(x):
    hi, lo = split(x)
    return jnp.concatenate([hi, hi, lo], 1)


def dot(a, b):
    return jnp.dot(a, b, preferred_element_type=f32)


def parts_of(z):
    n = z.shape[0] // 2
    return z[:n], z[n:]


def cmul(a, b):
    (ar, ai), (br, bi) = parts_of(a), parts_of(b)
    return jnp.concatenate([ar * br - ai * bi, ar * bi + ai * br], 0)


def cmul_conj(a, b):
    (ar, ai), (br, bi) = parts_of(a), parts_of(b)
    return jnp.concatenate([ar * br + ai * bi, ar * bi - ai * br], 0)


def turned(z):
    q = z.shape[0] // 4
    return jnp.concatenate([z[2 * q : 3 * q], -z[3 * q :], -z[:q], z[q : 2 * q]], 0)


def add_turned(y, z):
    q = z.shape[0] // 4
    return jnp.concatenate(
        [
            y[:q] + z[2 * q : 3 * q],
            y[q : 2 * q] - z[3 * q :],
            y[2 * q : 3 * q] - z[:q],
            y[3 * q :] + z[q : 2 * q],
        ],
        0,
    )


def conj_turned(w, z):
    n = w.shape[0] // 2
    h = n // 2
    wr, wi, zr, zi = w[:n], w[n:], z[:n], z[n:]
    re = wr * zi - wi * zr
    im = wr * zr + wi * zi
    return jnp.concatenate([re[:h], -re[h:], -im[:h], im[h:]], 0)


def kernel(
    size, factor,
    q1_in, k1_in, v1_in, q2_in, k2_in, co_in, taps_in, rates, res_in, tf_in, th_in, tn_in, ti_in,
    gq1, gk1, gv1, gq2, gk2, taps_st, res_st,
    q1, k1, v1, q2, k2, co, taps, res, tf, thr, thf, tn, ti,
    rise_t, ms_t, mst_t, lead_t, tail_t,
    lspec, kback, tspec, fspec, wone, mr_one, lback, lconv, ctail,
    bstate, bpeer, bsum, bslots, fstate, fpeer, fsum, fslots, halo_k, halo_v, chead, cnext,
    part, xch, got, gat, sib,
    in_sem, bp_send, bp_recv, bs_send, bs_recv, fp_send, fp_recv, fs_send, fs_recv,
    hf_send, hf_recv, hb_send, hb_recv,
    x_send, x_recv, r_send, r_recv, g_send, g_recv, s_send, s_recv,
):
    length, channels = q1.shape
    ntaps = taps.shape[0]
    modes = res.shape[0]
    groups = channels // (2 * WIDE)
    chips = size // 2
    slots, steps = part.shape[2], chips.bit_length() - 1
    lanes = WIDE // 128
    me = lax.axis_index("ctx")
    core, chip = lax.rem(me, 2), me // 2
    peer = me + 1 - 2 * core

    barrier = pltpu.get_barrier_semaphore()
    for k in range(1, size):
        pl.semaphore_signal(
            barrier, inc=1, device_id={"ctx": lax.rem(me + k, size)},
            device_id_type=pl.DeviceIdType.MESH,
        )

    loads = []
    for n, (src, dst) in enumerate(
        [
            (q2_in, q2), (co_in, co), (th_in, thr.at[pl.ds(0, 2 * ntaps)]), (th_in, thf.at[pl.ds(0, 2 * ntaps)]),
            (tn_in, tn), (res_in, res), (taps_in, taps), (tf_in, tf), (ti_in, ti),
            (k1_in, k1), (v1_in, v1), (q1_in, q1), (k2_in, k2),
        ]
    ):
        copy = pltpu.make_async_copy(src, dst, in_sem.at[n])
        copy.start()
        loads.append(copy)

    def remote(src, dst, send, recv, target):
        return pltpu.make_async_remote_copy(
            src_ref=src, dst_ref=dst, send_sem=send, recv_sem=recv,
            device_id={"ctx": target}, device_id_type=pl.DeviceIdType.MESH,
        )

    def wide_cols(g):
        return pl.ds(pl.multiple_of(g * 2 * WIDE, 2 * WIDE), 2 * WIDE)

    def rate_at(shape, dim):
        at = lax.rem(lax.broadcasted_iota(jnp.int32, shape, dim), modes)
        out = jnp.zeros(shape, f32)
        for m in range(modes):
            out = jnp.where(at == m, rates[m], out)
        return out

    def scale_of(rate):
        x = 2.0 * rate
        tail = 1.0 - x * (1.0 / 8.0)
        for n in range(7, 1, -1):
            tail = 1.0 - x * (1.0 / n) * tail
        return jnp.sqrt(x * tail)

    def iota(shape, dim):
        return lax.broadcasted_iota(jnp.int32, shape, dim)

    def first_rows(x):
        return jnp.where(iota(x.shape, 0) < modes, x, 0.0)

    def lane_parts(x):
        hi = x.astype(bf16).astype(f32)
        at = iota(x.shape, 1) // modes
        return jnp.where(at < 2, hi, jnp.where(at == 2, x - hi, 0.0)).astype(bf16)

    rows_long = rate_at((2 * modes, length), 0)
    places = iota((2 * modes, length), 1).astype(f32)
    rise_t[...] = three_lanes(first_rows(jnp.exp(-rows_long * places)))

    @pl.when(me == 0)
    def _():
        halo_k[...] = jnp.zeros_like(halo_k)
        halo_v[...] = jnp.zeros_like(halo_v)

    @pl.when(me == size - 1)
    def _():
        cnext[...] = jnp.zeros_like(cnext)

    @pl.when(core == 0)
    def _():
        fpeer[...] = jnp.zeros_like(fpeer)

    @pl.when(core == 1)
    def _():
        bpeer[...] = jnp.zeros_like(bpeer)

    for j in range(1, chips):
        @pl.when(chip + j >= chips)
        def _():
            bslots[j - 1] = jnp.zeros_like(bstate)

        @pl.when(chip - j < 0)
        def _():
            fslots[:, j - 1] = jnp.zeros((groups, modes, 2 * WIDE), f32)

    if part.shape[2] > (ntaps + modes) // 8 * lanes:
        used = (ntaps + modes) // 8 * lanes
        part[:, :, used:] = jnp.zeros((groups, 2, slots - used, 8, 128), f32)

    loads[0].wait()
    loads[1].wait()

    def first(g, carry):
        at = wide_cols(g)
        cotan = co[:, at].astype(f32) * q2[:, at].astype(f32)
        bstate[:, at] = dot(rise_t[...], three(cotan))[:modes]
        return carry

    lax.fori_loop(0, groups, first, 0)
    pl.semaphore_wait(barrier, size - 1)

    def back_peer():
        return remote(bstate, bpeer, bp_send, bp_recv, peer)

    def back_state(j, q, other):
        return remote(bsum, bslots.at[j - 1], bs_send.at[j - 1, q], bs_recv.at[j - 1], 2 * other + q)

    @pl.when(core == 1)
    def _():
        back_peer().start()

    def halo_copies(g, target):
        rows = pl.ds(length - ntaps, ntaps)
        return (
            remote(k1_in.at[rows, wide_cols(g)], halo_k.at[g], hf_send.at[0, g], hf_recv.at[0, g], target),
            remote(v1_in.at[rows, wide_cols(g)], halo_v.at[g], hf_send.at[1, g], hf_recv.at[1, g], target),
        )

    @pl.when(me + 1 < size)
    def _():
        for g in range(groups):
            for copy in halo_copies(g, me + 1):
                copy.start()

    for copy in loads[2:5]:
        copy.wait()

    rows_short = rate_at((2 * modes, ntaps), 0)
    places = iota((2 * modes, ntaps), 1).astype(f32)
    thr[2 * ntaps :] = three_lanes(first_rows(jnp.exp(-rows_short * places)))
    thf[2 * ntaps :] = three_lanes(first_rows(jnp.exp(-rows_short * (ntaps - 1.0 - places))))
    scaled = first_rows(scale_of(rows_short) * jnp.exp(-rows_short * places))
    back_table = jnp.concatenate(
        [tn[:, : 2 * ntaps], tn[:, 4 * ntaps :], tn[:, : 2 * ntaps]], 0
    )
    unit = 1.0 / ntaps
    mst_t[...] = three_lanes((unit * factor) * dot(three_lanes(scaled), back_table))
    lane_rate = rate_at((ntaps, 4 * modes), 1)
    places = iota((ntaps, 4 * modes), 0).astype(f32)
    lane_scale = scale_of(lane_rate)
    spread = dot(thr[: 2 * ntaps], three(lane_scale * jnp.exp(-lane_rate * places)))
    ms_t[...] = lane_parts(unit * spread)
    tail_t[...] = lane_parts(lane_scale * jnp.exp(-lane_rate * (ntaps - places)))
    lane_rate = rate_at((length, 4 * modes), 1)
    places = iota((length, 4 * modes), 0).astype(f32)
    lead_t[...] = lane_parts(scale_of(lane_rate) * jnp.exp(-lane_rate * (places + 1.0)))
    mode_rate = rate_at((modes, 2 * WIDE), 0)
    over_block = jnp.exp(-mode_rate * float(ntaps))
    over_device = jnp.exp(-mode_rate * float(length))
    over_chip = jnp.exp(-mode_rate * float(2 * length))

    @pl.when(core == 0)
    def _():
        back_peer().wait_recv()
        for g in range(groups):
            at = slice(2 * WIDE * g, 2 * WIDE * (g + 1))
            bsum[:, at] = bstate[:, at] + over_device * bpeer[:, at]
        for j in range(1, chips):
            @pl.when(chip - j >= 0)
            def _():
                for q in range(2):
                    back_state(j, q, chip - j).start()

    one_step = (factor * scale_of(mode_rate)) * jnp.exp(-mode_rate)
    nblocks = length // ntaps
    spec = 2 * ntaps

    blocks = [slice(b * ntaps, (b + 1) * ntaps) for b in range(nblocks)]
    across = 2 * WIDE

    def beside(arrays):
        return jnp.concatenate(arrays, 1)

    def apart(array):
        return [array[:, i : i + across] for i in range(0, array.shape[1], across)]

    def second(g, carry):
        at = wide_cols(g)
        cotan = co[:, at].astype(f32) * q2[:, at].astype(f32)
        mixed = k1[:, at].astype(f32) * v1[:, at].astype(f32)
        w = dot(tf[...], three(mixed))
        wone[:, at] = w
        fs = dot(ms_t[...], three_small(res[:, at]))
        fspec[:, at] = fs
        both = apart(dot(thr[...], beside([three(cotan[rows]) for rows in blocks] + [three(taps[:, at] * unit)])))
        ts = both[nblocks][:spec]
        tspec[:, at] = ts
        for b in range(nblocks):
            lspec[b, :, at] = both[b][:spec]
            kback[b, :, at] = both[b][spec : spec + modes]
        mr_one[:, at] = dot(ti[...], three(cmul(ts, w)))
        near = apart(dot(tn[...], beside([three(cmul_conj(fs, both[b][:spec])) for b in range(nblocks)])))
        for b in range(nblocks):
            lback[blocks[b], at] = near[b]
        return carry

    for copy in loads[5:]:
        copy.wait()

    lax.fori_loop(0, groups, second, 0)

    for j in range(1, chips):
        @pl.when(chip + j < chips)
        def _():
            back_state(j, core, chip + j).wait_recv()

    def cot_copy(g, target):
        return remote(chead.at[g], cnext.at[g], hb_send.at[g], hb_recv.at[g], target)

    def front_peer(g):
        return remote(fstate.at[g], fpeer.at[g], fp_send.at[g], fp_recv.at[g], peer)

    def front_copy(g, j, q, other):
        return remote(
            fsum.at[g], fslots.at[g, j - 1], fs_send.at[g, j - 1, q], fs_recv.at[g, j - 1], 2 * other + q
        )

    def front_out(g):
        @pl.when(core == 1)
        def _():
            front_peer(g).wait_recv()
            fsum[g] = over_device * fpeer[g] + fstate[g]
            for j in range(1, chips):
                @pl.when(chip + j < chips)
                def _():
                    for q in range(2):
                        front_copy(g, j, q, chip + j).start()

    def third(g):
        at = wide_cols(g)
        r = res[:, at]
        ts, fs = tspec[:, at], fspec[:, at]
        cotan = co[:, at].astype(f32)
        key_li, query = k2[:, at].astype(f32), q1[:, at].astype(f32)
        state = bslots[chips - 2, :, at]
        for j in range(chips - 2, 0, -1):
            state = over_chip * state + bslots[j - 1, :, at]
        state = jnp.where(core == 0, bpeer[:, at] + over_device * state, state)
        later = [over_block * state + kback[1, :, at], state]
        far = apart(dot(tail_t[...], beside([three_small(r * later[b]) for b in range(nblocks)])))
        prior = halo_k[g].astype(f32) * halo_v[g].astype(f32)
        mixed = k1[:ntaps, at].astype(f32) * v1[:ntaps, at].astype(f32)
        w0 = dot(tf[...], three(jnp.concatenate([prior, mixed], 0)))
        back = lback[:, at] + jnp.concatenate(far, 0)
        mr_grad = cotan + key_li * back
        grad = mr_grad * query
        hi, lo = split(grad)
        chead[g, 0] = hi[:ntaps]
        chead[g, 1] = lo[:ntaps]

        @pl.when(me > 0)
        def _():
            cot_copy(g, me - 1).start()

        mr0 = dot(ti[...], three(cmul(ts, w0)))
        cs = apart(dot(thr[:spec], beside([jnp.concatenate([hi[rows], lo[rows], hi[rows]], 0) for rows in blocks])))
        ctail[:, at] = cs[1]
        w1 = wone[:, at]
        mr = jnp.concatenate([mr0, mr_one[:, at]], 0)
        gq1[:, at] = (mr_grad * mr).astype(bf16)
        mr_out = query * mr
        gk2[:, at] = (mr_out * back).astype(bf16)
        x = key_li * mr_out
        both = apart(dot(thf[...], beside([three(x[rows]) for rows in blocks])))
        turn = conj_turned(w0, cs[0]) + conj_turned(w1, cs[1])
        taps_part, mg = apart(dot(tn[...], beside([three(turn), three(cmul_conj(ts, add_turned(cs[0], cs[1])))])))
        taps_part = taps_part * (unit * factor)
        for p in range(2):
            for i in range(ntaps // 8):
                for j in range(lanes):
                    lane = p * WIDE + 128 * j
                    part[g, p, i * lanes + j] = taps_part[8 * i : 8 * i + 8, lane : lane + 128]
        gk1[:ntaps, at] = (mg * v1[:ntaps, at].astype(f32)).astype(bf16)
        gv1[:ntaps, at] = (mg * k1[:ntaps, at].astype(f32)).astype(bf16)

        fronts = [both[b][spec : spec + modes] for b in range(nblocks)]
        fstate[g] = over_block * fronts[0] + fronts[1]
        lag = cmul_conj(both[0][:spec], lspec[0, :, at]) + cmul_conj(both[1][:spec], lspec[1, :, at])
        near = apart(dot(tn[...], beside([three(cmul(fs, both[b][:spec])) for b in range(nblocks)])))
        near[1] = near[1] + dot(lead_t[:ntaps], three_small(r * fronts[0]))
        for b in range(nblocks):
            lconv[blocks[b], at] = near[b]
        res_part = dot(mst_t[...], three(lag))[:modes]
        res_part = res_part + one_step * (fronts[0] * later[0] + fronts[1] * later[1])
        for p in range(2):
            for j in range(lanes):
                lane = p * WIDE + 128 * j
                part[g, p, ntaps // 8 * lanes + j] = res_part[:, lane : lane + 128]

    def fourth(g):
        at = wide_cols(g)
        state = fslots[g, chips - 2]
        for j in range(chips - 2, 0, -1):
            state = over_chip * state + fslots[g, j - 1]
        state = jnp.where(core == 1, fpeer[g] + over_device * state, state)
        hi, lo = cnext[g, 0], cnext[g, 1]
        nxt = dot(thr[:spec], jnp.concatenate([hi, lo, hi], 0))
        conv = lconv[:, at] + dot(lead_t[...], three_small(res[:, at] * state))
        gq2[:, at] = (co[:, at].astype(f32) * conv).astype(bf16)
        mg = dot(tn[...], three(cmul_conj(tspec[:, at], add_turned(ctail[:, at], nxt))))
        gk1[ntaps:, at] = (mg * v1[ntaps:, at].astype(f32)).astype(bf16)
        gv1[ntaps:, at] = (mg * k1[ntaps:, at].astype(f32)).astype(bf16)

    def to_peer(g):
        return remote(part.at[g, 1 - core], xch.at[g], x_send.at[g], x_recv.at[g], peer)

    def side(i):
        return lax.rem(chip // (chips >> (i + 1)), 2)

    def partner(i):
        return me + (1 - 2 * side(i)) * 2 * (chips >> (i + 1))

    def low(i):
        return sum([side(k) * (slots >> (k + 1)) for k in range(i)], 0)

    def kept(i):
        return pl.ds(low(i + 1), slots >> (i + 1))

    def landed(i):
        return pl.ds(slots - (slots >> i), slots >> (i + 1))

    def scatter(g, i):
        sent = pl.ds(low(i) + (1 - side(i)) * (slots >> (i + 1)), slots >> (i + 1))
        return remote(
            part.at[g, core, sent], got.at[g, landed(i)], r_send.at[g, i], r_recv.at[g, i], partner(i)
        )

    def gather(g, i):
        return remote(gat.at[g, kept(i)], gat.at[g, kept(i)], g_send.at[g, i], g_recv.at[g, i], partner(i))

    def to_sib(g):
        return remote(gat.at[g], sib.at[g], s_send.at[g], s_recv.at[g], peer)

    def stage_peer(g):
        to_peer(g).wait_recv()
        part[g, core] = part[g, core] + xch[g]
        scatter(g, 0).start()
        front_out(g)

    def stage_scatter(i):
        def stage(g):
            scatter(g, i).wait_recv()
            total = part[g, core, kept(i)] + got[g, landed(i)]
            if i < steps - 1:
                part[g, core, kept(i)] = total
                scatter(g, i + 1).start()
            else:
                gat[g, kept(i)] = total
                gather(g, i).start()

        return stage

    def stage_gather(i):
        def stage(g):
            gather(g, i).wait_recv()
            if i > 0:
                gather(g, i - 1).start()
            else:
                to_sib(g).start()

        return stage

    def stage_last(g):
        to_sib(g).wait_recv()
        for src, half in ((gat, core), (sib, 1 - core)):
            for j in range(lanes):
                at = pl.ds(pl.multiple_of((2 * g + half) * WIDE + 128 * j, 128), 128)
                for i in range(ntaps // 8):
                    taps_st[8 * i : 8 * i + 8, at] = src[g, i * lanes + j]
                res_st[:, at] = src[g, ntaps // 8 * lanes + j]

    ordered = [stage_peer]
    ordered += [stage_scatter(i) for i in range(steps)]
    ordered += [stage_gather(i) for i in reversed(range(steps))]
    ordered += [stage_last]

    def stages(s):
        for n, stage in enumerate(ordered):
            g = s - (n + 1)

            @pl.when((g >= 0) & (g < groups))
            def _():
                stage(g)

    def third_group(g, carry):
        @pl.when(me > 0)
        def _():
            for copy in halo_copies(g, me - 1):
                copy.wait_recv()

        third(g)
        to_peer(g).start()

        @pl.when(core == 0)
        def _():
            front_peer(g).start()

        stages(g)
        return carry

    lax.fori_loop(0, groups, third_group, 0)

    def fourth_group(s, carry):
        g = s - groups

        @pl.when(g < groups)
        def _():
            for j in range(1, chips):
                @pl.when(chip - j >= 0)
                def _():
                    front_copy(g, j, core, chip - j).wait_recv()

            @pl.when(me + 1 < size)
            def _():
                cot_copy(g, me + 1).wait_recv()

            fourth(g)

        stages(s)
        return carry

    lax.fori_loop(groups, groups + max(groups, len(ordered)), fourth_group, 0)

    @pl.when(core == 1)
    def _():
        back_peer().wait_send()

    for j in range(1, chips):
        @pl.when((core == 0) & (chip - j >= 0))
        def _():
            for q in range(2):
                back_state(j, q, chip - j).wait_send()

    def finish(g, carry):
        @pl.when(me + 1 < size)
        def _():
            for copy in halo_copies(g, me + 1):
                copy.wait_send()

        @pl.when(me > 0)
        def _():
            cot_copy(g, me - 1).wait_send()

        @pl.when(core == 0)
        def _():
            front_peer(g).wait_send()

        for j in range(1, chips):
            @pl.when((core == 1) & (chip + j < chips))
            def _():
                for q in range(2):
                    front_copy(g, j, q, chip + j).wait_send()

        to_peer(g).wait_send()
        to_sib(g).wait_send()
        for i in range(steps):
            scatter(g, i).wait_send()
            gather(g, i).wait_send()
        return carry

    lax.fori_loop(0, groups, finish, 0)


def write_out(*refs):
    copies = [pltpu.make_async_copy(refs[i], refs[7 + i], refs[14].at[i]) for i in range(7)]
    for copy in copies:
        copy.start()
    for copy in copies:
        copy.wait()


def per_device(q1, k1, v1, q2, k2, co, mr_taps, decay_rates, residues):
    size = lax.axis_size("ctx")
    length, channels = q1.shape
    ntaps, modes = mr_taps.shape[0], residues.shape[0]
    groups, chips = channels // (2 * WIDE), size // 2
    steps = chips.bit_length() - 1
    nblocks, spec = length // ntaps, 2 * ntaps
    used = (ntaps + modes) // 8 * (WIDE // 128)
    share = -(-used // chips)
    slots = share * chips
    factor = 1.0 / math.sqrt(length * size)
    consts = [jnp.asarray(t) for t in tables(ntaps)]

    def vm(*shape, dtype=f32):
        return pltpu.VMEM(shape, dtype)

    dma = lambda *shape: pltpu.SemaphoreType.DMA(shape)
    wide = lambda: vm(length, channels, dtype=bf16)
    scratch = [
        wide(), wide(), wide(), wide(), wide(), wide(),
        vm(ntaps, channels), vm(modes, channels),
        vm(spec, 3 * spec, dtype=bf16), vm(spec + 2 * modes, 3 * ntaps, dtype=bf16),
        vm(spec + 2 * modes, 3 * ntaps, dtype=bf16),
        vm(ntaps, 3 * spec, dtype=bf16), vm(ntaps, 3 * spec, dtype=bf16),
        vm(2 * modes, 3 * length, dtype=bf16), vm(spec, 4 * modes, dtype=bf16),
        vm(2 * modes, 3 * spec, dtype=bf16), vm(length, 4 * modes, dtype=bf16),
        vm(ntaps, 4 * modes, dtype=bf16),
        vm(nblocks, spec, channels), vm(nblocks, modes, channels), vm(spec, channels), vm(spec, channels),
        vm(spec, channels), vm(ntaps, channels), vm(length, channels), vm(length, channels),
        vm(spec, channels),
        vm(modes, channels), vm(modes, channels), vm(modes, channels), vm(chips - 1, modes, channels),
        vm(groups, modes, 2 * WIDE), vm(groups, modes, 2 * WIDE), vm(groups, modes, 2 * WIDE),
        vm(groups, chips - 1, modes, 2 * WIDE),
        vm(groups, ntaps, 2 * WIDE, dtype=bf16), vm(groups, ntaps, 2 * WIDE, dtype=bf16),
        vm(groups, 2, ntaps, 2 * WIDE, dtype=bf16), vm(groups, 2, ntaps, 2 * WIDE, dtype=bf16),
        vm(groups, 2, slots, 8, 128), vm(groups, slots, 8, 128), vm(groups, slots, 8, 128),
        vm(groups, slots, 8, 128), vm(groups, slots, 8, 128),
        dma(13), pltpu.SemaphoreType.DMA, pltpu.SemaphoreType.DMA, dma(chips - 1, 2), dma(chips - 1),
        dma(groups), dma(groups), dma(groups, chips - 1, 2), dma(groups, chips - 1),
        dma(2, groups), dma(2, groups), dma(groups), dma(groups),
        dma(groups), dma(groups), dma(groups, steps), dma(groups, steps),
        dma(groups, steps), dma(groups, steps), dma(groups), dma(groups),
    ]
    anywhere = pl.BlockSpec(memory_space=pl.ANY)
    specs = [anywhere] * 7 + [pl.BlockSpec(memory_space=pltpu.SMEM)] + [anywhere] * 5
    results = [((length, channels), bf16)] * 5 + [((ntaps, channels), f32), ((modes, channels), f32)]
    held = pl.pallas_call(
        lambda *refs: kernel(size, factor, *refs),
        out_shape=tuple(pltpu.VMEM(*r) for r in results),
        in_specs=specs,
        out_specs=(pl.BlockSpec(memory_space=pltpu.VMEM),) * 7,
        scratch_shapes=scratch,
        compiler_params=pltpu.CompilerParams(
            collective_id=0, has_side_effects=True, vmem_limit_bytes=50 * 2**20
        ),
        name="backward",
    )(q1, k1, v1, q2, k2, co, mr_taps, decay_rates, residues, *consts)
    held = [pltpu.with_memory_space_constraint(x, pltpu.VMEM) for x in held]
    return pl.pallas_call(
        write_out,
        out_shape=tuple(jax.ShapeDtypeStruct(*r) for r in results),
        in_specs=(pl.BlockSpec(memory_space=pltpu.VMEM),) * 7,
        out_specs=(anywhere,) * 7,
        scratch_shapes=[dma(7)],
        compiler_params=pltpu.CompilerParams(vmem_limit_bytes=2**20),
        name="write_out",
    )(*held)


def solution(mesh):
    whole, cols = P("ctx", "tp"), P(None, "tp")
    return jax.shard_map(
        per_device,
        mesh=mesh,
        in_specs=(whole,) * 6 + (cols, P(), cols),
        out_specs=(whole,) * 5 + (cols, cols),
        check_vma=False,
    )
```

```python
import math

import numpy as np
import ml_dtypes
import jax
import jax.numpy as jnp
from jax import lax
from jax.experimental import pallas as pl
from jax.experimental.pallas import tpu as pltpu
from jax.sharding import PartitionSpec as P

f32, bf16 = jnp.float32, jnp.bfloat16
WIDE = 256


def tables(taps):
    size, half = 2 * taps, taps // 2
    order = np.concatenate([np.arange(0, taps, 2), np.arange(1, taps, 2)])
    angle = (2.0 * np.pi / size) * (order[:, None] + 0.5) * np.arange(size)[None, :]
    full = np.concatenate([np.cos(angle), -np.sin(angle)], 0)

    def three(table):
        hi = table.astype(ml_dtypes.bfloat16)
        lo = (table - hi.astype(np.float64)).astype(ml_dtypes.bfloat16)
        return np.concatenate([hi, hi, lo], 1)

    return (
        three(full),
        three(full[:, :taps]),
        three(full[:, :taps].T),
        three(full[:, taps:].T),
    )


def split(x):
    hi = x.astype(bf16)
    return hi, (x - hi.astype(f32)).astype(bf16)


def three(x):
    hi, lo = split(x)
    return jnp.concatenate([hi, lo, hi], 0)


def three_small(x):
    hi = x.astype(bf16).astype(f32)
    return jnp.concatenate([hi, x - hi, hi, jnp.zeros_like(x)], 0).astype(bf16)


def three_lanes(x):
    hi, lo = split(x)
    return jnp.concatenate([hi, hi, lo], 1)


def dot(a, b):
    return jnp.dot(a, b, preferred_element_type=f32)


def parts_of(z):
    n = z.shape[0] // 2
    return z[:n], z[n:]


def cmul(a, b):
    (ar, ai), (br, bi) = parts_of(a), parts_of(b)
    return jnp.concatenate([ar * br - ai * bi, ar * bi + ai * br], 0)


def cmul_conj(a, b):
    (ar, ai), (br, bi) = parts_of(a), parts_of(b)
    return jnp.concatenate([ar * br + ai * bi, ar * bi - ai * br], 0)


def turned(z):
    q = z.shape[0] // 4
    return jnp.concatenate([z[2 * q : 3 * q], -z[3 * q :], -z[:q], z[q : 2 * q]], 0)


def add_turned(y, z):
    q = z.shape[0] // 4
    return jnp.concatenate(
        [
            y[:q] + z[2 * q : 3 * q],
            y[q : 2 * q] - z[3 * q :],
            y[2 * q : 3 * q] - z[:q],
            y[3 * q :] + z[q : 2 * q],
        ],
        0,
    )


def conj_turned(w, z):
    n = w.shape[0] // 2
    h = n // 2
    wr, wi, zr, zi = w[:n], w[n:], z[:n], z[n:]
    re = wr * zi - wi * zr
    im = wr * zr + wi * zi
    return jnp.concatenate([re[:h], -re[h:], -im[:h], im[h:]], 0)


def kernel(
    size, factor,
    q1_in, k1_in, v1_in, q2_in, k2_in, co_in, taps_in, rates, res_in, tf_in, th_in, tn_in, ti_in,
    gq1, gk1, gv1, gq2, gk2, taps_st, res_st,
    q1, k1, v1, q2, k2, co, taps, res, tf, thr, thf, tn, ti,
    rise_t, ms_t, mst_t, lead_t, tail_t,
    lspec, kback, tspec, fspec, wone, mr_one, lback, ctail,
    bstate, bpeer, bsum, bslots, fstate, fpeer, fsum, fslots, halo_k, halo_v, chead, cnext,
    part, xch, got, gat, sib,
    in_sem, bp_send, bp_recv, bs_send, bs_recv, fp_send, fp_recv, fs_send, fs_recv,
    hf_send, hf_recv, hb_send, hb_recv,
    x_send, x_recv, r_send, r_recv, g_send, g_recv, s_send, s_recv,
):
    length, channels = q1.shape
    ntaps = taps.shape[0]
    modes = res.shape[0]
    groups = channels // (2 * WIDE)
    chips = size // 2
    slots, steps = part.shape[2], chips.bit_length() - 1
    lanes = WIDE // 128
    me = lax.axis_index("ctx")
    core, chip = lax.rem(me, 2), me // 2
    peer = me + 1 - 2 * core

    barrier = pltpu.get_barrier_semaphore()
    for k in range(1, size):
        pl.semaphore_signal(
            barrier, inc=1, device_id={"ctx": lax.rem(me + k, size)},
            device_id_type=pl.DeviceIdType.MESH,
        )

    loads = []
    for n, (src, dst) in enumerate(
        [
            (q2_in, q2), (co_in, co), (th_in, thr.at[pl.ds(0, 2 * ntaps)]), (th_in, thf.at[pl.ds(0, 2 * ntaps)]),
            (tn_in, tn), (res_in, res), (taps_in, taps), (tf_in, tf), (ti_in, ti),
            (k1_in, k1), (v1_in, v1), (q1_in, q1), (k2_in, k2),
        ]
    ):
        copy = pltpu.make_async_copy(src, dst, in_sem.at[n])
        copy.start()
        loads.append(copy)

    def remote(src, dst, send, recv, target):
        return pltpu.make_async_remote_copy(
            src_ref=src, dst_ref=dst, send_sem=send, recv_sem=recv,
            device_id={"ctx": target}, device_id_type=pl.DeviceIdType.MESH,
        )

    def wide_cols(g):
        return pl.ds(pl.multiple_of(g * 2 * WIDE, 2 * WIDE), 2 * WIDE)

    def rate_at(shape, dim):
        at = lax.rem(lax.broadcasted_iota(jnp.int32, shape, dim), modes)
        out = jnp.zeros(shape, f32)
        for m in range(modes):
            out = jnp.where(at == m, rates[m], out)
        return out

    def scale_of(rate):
        x = 2.0 * rate
        tail = 1.0 - x * (1.0 / 8.0)
        for n in range(7, 1, -1):
            tail = 1.0 - x * (1.0 / n) * tail
        return jnp.sqrt(x * tail)

    def iota(shape, dim):
        return lax.broadcasted_iota(jnp.int32, shape, dim)

    def first_rows(x):
        return jnp.where(iota(x.shape, 0) < modes, x, 0.0)

    def lane_parts(x):
        hi = x.astype(bf16).astype(f32)
        at = iota(x.shape, 1) // modes
        return jnp.where(at < 2, hi, jnp.where(at == 2, x - hi, 0.0)).astype(bf16)

    rows_long = rate_at((2 * modes, length), 0)
    places = iota((2 * modes, length), 1).astype(f32)
    rise_t[...] = three_lanes(first_rows(jnp.exp(-rows_long * places)))

    @pl.when(me == 0)
    def _():
        halo_k[...] = jnp.zeros_like(halo_k)
        halo_v[...] = jnp.zeros_like(halo_v)

    @pl.when(me == size - 1)
    def _():
        cnext[...] = jnp.zeros_like(cnext)

    @pl.when(core == 0)
    def _():
        fpeer[...] = jnp.zeros_like(fpeer)

    @pl.when(core == 1)
    def _():
        bpeer[...] = jnp.zeros_like(bpeer)

    for j in range(1, chips):
        @pl.when(chip + j >= chips)
        def _():
            bslots[j - 1] = jnp.zeros_like(bstate)

        @pl.when(chip - j < 0)
        def _():
            fslots[:, j - 1] = jnp.zeros((groups, modes, 2 * WIDE), f32)

    if part.shape[2] > (ntaps + modes) // 8 * lanes:
        used = (ntaps + modes) // 8 * lanes
        part[:, :, used:] = jnp.zeros((groups, 2, slots - used, 8, 128), f32)

    loads[0].wait()
    loads[1].wait()

    def first(g, carry):
        at = wide_cols(g)
        cotan = co[:, at].astype(f32) * q2[:, at].astype(f32)
        bstate[:, at] = dot(rise_t[...], three(cotan))[:modes]
        return carry

    lax.fori_loop(0, groups, first, 0)
    pl.semaphore_wait(barrier, size - 1)

    def back_peer():
        return remote(bstate, bpeer, bp_send, bp_recv, peer)

    def back_state(j, q, other):
        return remote(bsum, bslots.at[j - 1], bs_send.at[j - 1, q], bs_recv.at[j - 1], 2 * other + q)

    @pl.when(core == 1)
    def _():
        back_peer().start()

    def halo_copies(g, target):
        rows = pl.ds(length - ntaps, ntaps)
        return (
            remote(k1_in.at[rows, wide_cols(g)], halo_k.at[g], hf_send.at[0, g], hf_recv.at[0, g], target),
            remote(v1_in.at[rows, wide_cols(g)], halo_v.at[g], hf_send.at[1, g], hf_recv.at[1, g], target),
        )

    @pl.when(me + 1 < size)
    def _():
        for g in range(groups):
            for copy in halo_copies(g, me + 1):
                copy.start()

    for copy in loads[2:5]:
        copy.wait()

    rows_short = rate_at((2 * modes, ntaps), 0)
    places = iota((2 * modes, ntaps), 1).astype(f32)
    thr[2 * ntaps :] = three_lanes(first_rows(jnp.exp(-rows_short * places)))
    thf[2 * ntaps :] = three_lanes(first_rows(jnp.exp(-rows_short * (ntaps - 1.0 - places))))
    scaled = first_rows(scale_of(rows_short) * jnp.exp(-rows_short * places))
    back_table = jnp.concatenate(
        [tn[:, : 2 * ntaps], tn[:, 4 * ntaps :], tn[:, : 2 * ntaps]], 0
    )
    unit = 1.0 / ntaps
    mst_t[...] = three_lanes((unit * factor) * dot(three_lanes(scaled), back_table))
    lane_rate = rate_at((ntaps, 4 * modes), 1)
    places = iota((ntaps, 4 * modes), 0).astype(f32)
    lane_scale = scale_of(lane_rate)
    spread = dot(thr[: 2 * ntaps], three(lane_scale * jnp.exp(-lane_rate * places)))
    ms_t[...] = lane_parts(unit * spread)
    tail_t[...] = lane_parts(lane_scale * jnp.exp(-lane_rate * (ntaps - places)))
    lead_t[...] = lane_parts(lane_scale * jnp.exp(-lane_rate * (places + 1.0)))
    mode_rate = rate_at((modes, 2 * WIDE), 0)
    over_block = jnp.exp(-mode_rate * float(ntaps))
    over_device = jnp.exp(-mode_rate * float(length))
    over_chip = jnp.exp(-mode_rate * float(2 * length))

    @pl.when(core == 0)
    def _():
        back_peer().wait_recv()
        for g in range(groups):
            at = slice(2 * WIDE * g, 2 * WIDE * (g + 1))
            bsum[:, at] = bstate[:, at] + over_device * bpeer[:, at]
        for j in range(1, chips):
            @pl.when(chip - j >= 0)
            def _():
                for q in range(2):
                    back_state(j, q, chip - j).start()

    one_step = (factor * scale_of(mode_rate)) * jnp.exp(-mode_rate)
    nblocks = length // ntaps
    spec = 2 * ntaps

    blocks = [slice(b * ntaps, (b + 1) * ntaps) for b in range(nblocks)]
    across = 2 * WIDE

    def beside(arrays):
        return jnp.concatenate(arrays, 1)

    def apart(array):
        return [array[:, i : i + across] for i in range(0, array.shape[1], across)]

    def second(g, carry):
        at = wide_cols(g)
        cotan = co[:, at].astype(f32) * q2[:, at].astype(f32)
        mixed = k1[:, at].astype(f32) * v1[:, at].astype(f32)
        w = dot(tf[...], three(mixed))
        wone[:, at] = w
        fs = dot(ms_t[...], three_small(res[:, at]))
        fspec[:, at] = fs
        both = apart(dot(thr[...], beside([three(cotan[rows]) for rows in blocks] + [three(taps[:, at] * unit)])))
        ts = both[nblocks][:spec]
        tspec[:, at] = ts
        for b in range(nblocks):
            lspec[b, :, at] = both[b][:spec]
            kback[b, :, at] = both[b][spec : spec + modes]
        mr_one[:, at] = dot(ti[...], three(cmul(ts, w)))
        near = apart(dot(tn[...], beside([three(cmul_conj(fs, both[b][:spec])) for b in range(nblocks)])))
        for b in range(nblocks):
            lback[blocks[b], at] = near[b]
        return carry

    for copy in loads[5:]:
        copy.wait()

    lax.fori_loop(0, groups, second, 0)

    for j in range(1, chips):
        @pl.when(chip + j < chips)
        def _():
            back_state(j, core, chip + j).wait_recv()

    def cot_copy(g, target):
        return remote(chead.at[g], cnext.at[g], hb_send.at[g], hb_recv.at[g], target)

    def front_peer(g):
        return remote(fstate.at[g], fpeer.at[g], fp_send.at[g], fp_recv.at[g], peer)

    def front_copy(g, j, q, other):
        return remote(
            fsum.at[g], fslots.at[g, j - 1], fs_send.at[g, j - 1, q], fs_recv.at[g, j - 1], 2 * other + q
        )

    def front_out(g):
        @pl.when(core == 1)
        def _():
            front_peer(g).wait_recv()
            fsum[g] = over_device * fpeer[g] + fstate[g]
            for j in range(1, chips):
                @pl.when(chip + j < chips)
                def _():
                    for q in range(2):
                        front_copy(g, j, q, chip + j).start()

    def third(g):
        at = wide_cols(g)
        r = res[:, at]
        ts = tspec[:, at]
        cotan = co[:, at].astype(f32)
        key_li, query = k2[:, at].astype(f32), q1[:, at].astype(f32)
        state = bslots[chips - 2, :, at]
        for j in range(chips - 2, 0, -1):
            state = over_chip * state + bslots[j - 1, :, at]
        state = jnp.where(core == 0, bpeer[:, at] + over_device * state, state)
        later = [over_block * state + kback[1, :, at], state]
        far = apart(dot(tail_t[...], beside([three_small(r * later[b]) for b in range(nblocks)])))
        prior = halo_k[g].astype(f32) * halo_v[g].astype(f32)
        mixed = k1[:ntaps, at].astype(f32) * v1[:ntaps, at].astype(f32)
        w0 = dot(tf[...], three(jnp.concatenate([prior, mixed], 0)))
        back = lback[:, at] + jnp.concatenate(far, 0)
        mr_grad = cotan + key_li * back
        grad = mr_grad * query
        hi, lo = split(grad)
        chead[g, 0] = hi[:ntaps]
        chead[g, 1] = lo[:ntaps]

        @pl.when(me > 0)
        def _():
            cot_copy(g, me - 1).start()

        mr0 = dot(ti[...], three(cmul(ts, w0)))
        cs = apart(dot(thr[:spec], beside([jnp.concatenate([hi[rows], lo[rows], hi[rows]], 0) for rows in blocks])))
        ctail[:, at] = cs[1]
        w1 = wone[:, at]
        mr = jnp.concatenate([mr0, mr_one[:, at]], 0)
        gq1[:, at] = (mr_grad * mr).astype(bf16)
        mr_out = query * mr
        gk2[:, at] = (mr_out * back).astype(bf16)
        x = key_li * mr_out
        both = apart(dot(thf[...], beside([three(x[rows]) for rows in blocks])))
        turn = conj_turned(w0, cs[0]) + conj_turned(w1, cs[1])
        taps_part = dot(tn[...], three(turn)) * (unit * factor)
        wone[:, at] = add_turned(cs[0], cs[1])
        for p in range(2):
            for i in range(ntaps // 8):
                for j in range(lanes):
                    lane = p * WIDE + 128 * j
                    part[g, p, i * lanes + j] = taps_part[8 * i : 8 * i + 8, lane : lane + 128]
        fronts = [both[b][spec : spec + modes] for b in range(nblocks)]
        fstate[g] = over_block * fronts[0] + fronts[1]
        lag = cmul_conj(both[0][:spec], lspec[0, :, at]) + cmul_conj(both[1][:spec], lspec[1, :, at])
        for b in range(nblocks):
            lspec[b, :, at] = both[b][:spec]
        kback[0, :, at] = fronts[0]
        res_part = dot(mst_t[...], three(lag))[:modes]
        res_part = res_part + one_step * (fronts[0] * later[0] + fronts[1] * later[1])
        for p in range(2):
            for j in range(lanes):
                lane = p * WIDE + 128 * j
                part[g, p, ntaps // 8 * lanes + j] = res_part[:, lane : lane + 128]

    def fourth(g):
        at = wide_cols(g)
        state = fslots[g, chips - 2]
        for j in range(chips - 2, 0, -1):
            state = over_chip * state + fslots[g, j - 1]
        state = jnp.where(core == 1, fpeer[g] + over_device * state, state)
        hi, lo = cnext[g, 0], cnext[g, 1]
        nxt = dot(thr[:spec], jnp.concatenate([hi, lo, hi], 0))
        r, ts, fs = res[:, at], tspec[:, at], fspec[:, at]
        before = [state, over_block * state + kback[0, :, at]]
        far = apart(dot(lead_t[...], beside([three_small(r * before[b]) for b in range(nblocks)])))
        spectra = [cmul(fs, lspec[b, :, at]) for b in range(nblocks)]
        spectra += [cmul_conj(ts, wone[:, at]), cmul_conj(ts, add_turned(ctail[:, at], nxt))]
        near = apart(dot(tn[...], beside([three(y) for y in spectra])))
        for b in range(nblocks):
            rows = blocks[b]
            gq2[rows, at] = (co[rows, at].astype(f32) * (near[b] + far[b])).astype(bf16)
            mg = near[nblocks + b]
            gk1[rows, at] = (mg * v1[rows, at].astype(f32)).astype(bf16)
            gv1[rows, at] = (mg * k1[rows, at].astype(f32)).astype(bf16)

    def to_peer(g):
        return remote(part.at[g, 1 - core], xch.at[g], x_send.at[g], x_recv.at[g], peer)

    each = slots // chips
    sizes = (chips * (each - each // 2), chips * (each // 2))
    starts = (0, sizes[0])
    orders = (list(range(steps - 1, -1, -1)), [steps - 1 - (i + 1) % steps for i in range(steps)])

    def side(h, i):
        return lax.rem(chip // (1 << orders[h][i]), 2)

    def partner(h, i):
        return me + (1 - 2 * side(h, i)) * (2 << orders[h][i])

    def low(h, i):
        return sum([side(h, k) * (sizes[h] >> (k + 1)) for k in range(i)], starts[h])

    def kept(h, i):
        return pl.ds(low(h, i + 1), sizes[h] >> (i + 1))

    def landed(h, i):
        return pl.ds(starts[h] + sizes[h] - (sizes[h] >> i), sizes[h] >> (i + 1))

    def scatter(g, h, i):
        sent = pl.ds(low(h, i) + (1 - side(h, i)) * (sizes[h] >> (i + 1)), sizes[h] >> (i + 1))
        return remote(
            part.at[g, core, sent], got.at[g, landed(h, i)],
            r_send.at[g, h, i], r_recv.at[g, h, i], partner(h, i),
        )

    def gather(g, h, i):
        return remote(
            gat.at[g, kept(h, i)], gat.at[g, kept(h, i)],
            g_send.at[g, h, i], g_recv.at[g, h, i], partner(h, i),
        )

    def to_sib(g):
        return remote(gat.at[g], sib.at[g], s_send.at[g], s_recv.at[g], peer)

    def stage_peer(g):
        to_peer(g).wait_recv()
        part[g, core] = part[g, core] + xch[g]
        for h in range(2):
            scatter(g, h, 0).start()
        front_out(g)

    def stage_scatter(i):
        def stage(g):
            for h in range(2):
                scatter(g, h, i).wait_recv()
                total = part[g, core, kept(h, i)] + got[g, landed(h, i)]
                if i < steps - 1:
                    part[g, core, kept(h, i)] = total
                    scatter(g, h, i + 1).start()
                else:
                    gat[g, kept(h, i)] = total
                    gather(g, h, i).start()

        return stage

    def stage_gather(i):
        def stage(g):
            for h in range(2):
                gather(g, h, i).wait_recv()
                if i > 0:
                    gather(g, h, i - 1).start()
            if i == 0:
                to_sib(g).start()

        return stage

    def stage_last(g):
        to_sib(g).wait_recv()
        for src, half in ((gat, core), (sib, 1 - core)):
            for j in range(lanes):
                at = pl.ds(pl.multiple_of((2 * g + half) * WIDE + 128 * j, 128), 128)
                for i in range(ntaps // 8):
                    taps_st[8 * i : 8 * i + 8, at] = src[g, i * lanes + j]
                res_st[:, at] = src[g, ntaps // 8 * lanes + j]

    ordered = [stage_peer]
    ordered += [stage_scatter(i) for i in range(steps)]
    ordered += [stage_gather(i) for i in reversed(range(steps))]
    ordered += [stage_last]

    def stages(s):
        for n, stage in enumerate(ordered):
            g = s - (n + 1)

            @pl.when((g >= 0) & (g < groups))
            def _():
                stage(g)

    def third_group(g, carry):
        @pl.when(me > 0)
        def _():
            for copy in halo_copies(g, me - 1):
                copy.wait_recv()

        third(g)
        to_peer(g).start()

        @pl.when(core == 0)
        def _():
            front_peer(g).start()

        stages(g)
        return carry

    lax.fori_loop(0, groups, third_group, 0)

    def fourth_group(s, carry):
        g = s - groups

        @pl.when(g < groups)
        def _():
            for j in range(1, chips):
                @pl.when(chip - j >= 0)
                def _():
                    front_copy(g, j, core, chip - j).wait_recv()

            @pl.when(me + 1 < size)
            def _():
                cot_copy(g, me + 1).wait_recv()

            fourth(g)

        stages(s)
        return carry

    lax.fori_loop(groups, groups + max(groups, len(ordered)), fourth_group, 0)

    @pl.when(core == 1)
    def _():
        back_peer().wait_send()

    for j in range(1, chips):
        @pl.when((core == 0) & (chip - j >= 0))
        def _():
            for q in range(2):
                back_state(j, q, chip - j).wait_send()

    def finish(g, carry):
        @pl.when(me + 1 < size)
        def _():
            for copy in halo_copies(g, me + 1):
                copy.wait_send()

        @pl.when(me > 0)
        def _():
            cot_copy(g, me - 1).wait_send()

        @pl.when(core == 0)
        def _():
            front_peer(g).wait_send()

        for j in range(1, chips):
            @pl.when((core == 1) & (chip + j < chips))
            def _():
                for q in range(2):
                    front_copy(g, j, q, chip + j).wait_send()

        to_peer(g).wait_send()
        to_sib(g).wait_send()
        for h in range(2):
            for i in range(steps):
                scatter(g, h, i).wait_send()
                gather(g, h, i).wait_send()
        return carry

    lax.fori_loop(0, groups, finish, 0)


def write_out(*refs):
    copies = [pltpu.make_async_copy(refs[i], refs[7 + i], refs[14].at[i]) for i in range(7)]
    for copy in copies:
        copy.start()
    for copy in copies:
        copy.wait()


def per_device(q1, k1, v1, q2, k2, co, mr_taps, decay_rates, residues):
    size = lax.axis_size("ctx")
    length, channels = q1.shape
    ntaps, modes = mr_taps.shape[0], residues.shape[0]
    groups, chips = channels // (2 * WIDE), size // 2
    steps = chips.bit_length() - 1
    nblocks, spec = length // ntaps, 2 * ntaps
    used = (ntaps + modes) // 8 * (WIDE // 128)
    share = -(-used // chips)
    slots = share * chips
    factor = 1.0 / math.sqrt(length * size)
    consts = [jnp.asarray(t) for t in tables(ntaps)]

    def vm(*shape, dtype=f32):
        return pltpu.VMEM(shape, dtype)

    dma = lambda *shape: pltpu.SemaphoreType.DMA(shape)
    wide = lambda: vm(length, channels, dtype=bf16)
    scratch = [
        wide(), wide(), wide(), wide(), wide(), wide(),
        vm(ntaps, channels), vm(modes, channels),
        vm(spec, 3 * spec, dtype=bf16), vm(spec + 2 * modes, 3 * ntaps, dtype=bf16),
        vm(spec + 2 * modes, 3 * ntaps, dtype=bf16),
        vm(ntaps, 3 * spec, dtype=bf16), vm(ntaps, 3 * spec, dtype=bf16),
        vm(2 * modes, 3 * length, dtype=bf16), vm(spec, 4 * modes, dtype=bf16),
        vm(2 * modes, 3 * spec, dtype=bf16), vm(ntaps, 4 * modes, dtype=bf16),
        vm(ntaps, 4 * modes, dtype=bf16),
        vm(nblocks, spec, channels), vm(nblocks, modes, channels), vm(spec, channels), vm(spec, channels),
        vm(spec, channels), vm(ntaps, channels), vm(length, channels),
        vm(spec, channels),
        vm(modes, channels), vm(modes, channels), vm(modes, channels), vm(chips - 1, modes, channels),
        vm(groups, modes, 2 * WIDE), vm(groups, modes, 2 * WIDE), vm(groups, modes, 2 * WIDE),
        vm(groups, chips - 1, modes, 2 * WIDE),
        vm(groups, ntaps, 2 * WIDE, dtype=bf16), vm(groups, ntaps, 2 * WIDE, dtype=bf16),
        vm(groups, 2, ntaps, 2 * WIDE, dtype=bf16), vm(groups, 2, ntaps, 2 * WIDE, dtype=bf16),
        vm(groups, 2, slots, 8, 128), vm(groups, slots, 8, 128), vm(groups, slots, 8, 128),
        vm(groups, slots, 8, 128), vm(groups, slots, 8, 128),
        dma(13), pltpu.SemaphoreType.DMA, pltpu.SemaphoreType.DMA, dma(chips - 1, 2), dma(chips - 1),
        dma(groups), dma(groups), dma(groups, chips - 1, 2), dma(groups, chips - 1),
        dma(2, groups), dma(2, groups), dma(groups), dma(groups),
        dma(groups), dma(groups), dma(groups, 2, steps), dma(groups, 2, steps),
        dma(groups, 2, steps), dma(groups, 2, steps), dma(groups), dma(groups),
    ]
    anywhere = pl.BlockSpec(memory_space=pl.ANY)
    specs = [anywhere] * 7 + [pl.BlockSpec(memory_space=pltpu.SMEM)] + [anywhere] * 5
    results = [((length, channels), bf16)] * 5 + [((ntaps, channels), f32), ((modes, channels), f32)]
    held = pl.pallas_call(
        lambda *refs: kernel(size, factor, *refs),
        out_shape=tuple(pltpu.VMEM(*r) for r in results),
        in_specs=specs,
        out_specs=(pl.BlockSpec(memory_space=pltpu.VMEM),) * 7,
        scratch_shapes=scratch,
        compiler_params=pltpu.CompilerParams(
            collective_id=0, has_side_effects=True, vmem_limit_bytes=50 * 2**20
        ),
        name="backward",
    )(q1, k1, v1, q2, k2, co, mr_taps, decay_rates, residues, *consts)
    held = [pltpu.with_memory_space_constraint(x, pltpu.VMEM) for x in held]
    return pl.pallas_call(
        write_out,
        out_shape=tuple(jax.ShapeDtypeStruct(*r) for r in results),
        in_specs=(pl.BlockSpec(memory_space=pltpu.VMEM),) * 7,
        out_specs=(anywhere,) * 7,
        scratch_shapes=[dma(7)],
        compiler_params=pltpu.CompilerParams(vmem_limit_bytes=2**20),
        name="write_out",
    )(*held)


def solution(mesh):
    whole, cols = P("ctx", "tp"), P(None, "tp")
    return jax.shard_map(
        per_device,
        mesh=mesh,
        in_specs=(whole,) * 6 + (cols, P(), cols),
        out_specs=(whole,) * 5 + (cols, cols),
        check_vma=False,
    )
```

```python
import math

import numpy as np
import ml_dtypes
import jax
import jax.numpy as jnp
from jax import lax
from jax.experimental import pallas as pl
from jax.experimental.pallas import tpu as pltpu
from jax.sharding import PartitionSpec as P

f32, bf16 = jnp.float32, jnp.bfloat16
WIDE = 256


def tables(taps):
    size, half = 2 * taps, taps // 2
    order = np.concatenate([np.arange(0, taps, 2), np.arange(1, taps, 2)])
    angle = (2.0 * np.pi / size) * (order[:, None] + 0.5) * np.arange(size)[None, :]
    full = np.concatenate([np.cos(angle), -np.sin(angle)], 0)

    def three(table):
        hi = table.astype(ml_dtypes.bfloat16)
        lo = (table - hi.astype(np.float64)).astype(ml_dtypes.bfloat16)
        return np.concatenate([hi, hi, lo], 1)

    return (
        three(full),
        three(full[:, :taps]),
        three(full[:, :taps].T),
        three(full[:, taps:].T),
    )


def split(x):
    hi = x.astype(bf16)
    return hi, (x - hi.astype(f32)).astype(bf16)


def three(x):
    hi, lo = split(x)
    return jnp.concatenate([hi, lo, hi], 0)


def three_small(x):
    hi = x.astype(bf16).astype(f32)
    return jnp.concatenate([hi, x - hi, hi, jnp.zeros_like(x)], 0).astype(bf16)


def three_lanes(x):
    hi, lo = split(x)
    return jnp.concatenate([hi, hi, lo], 1)


def dot(a, b):
    return jnp.dot(a, b, preferred_element_type=f32)


def parts_of(z):
    n = z.shape[0] // 2
    return z[:n], z[n:]


def cmul(a, b):
    (ar, ai), (br, bi) = parts_of(a), parts_of(b)
    return jnp.concatenate([ar * br - ai * bi, ar * bi + ai * br], 0)


def cmul_conj(a, b):
    (ar, ai), (br, bi) = parts_of(a), parts_of(b)
    return jnp.concatenate([ar * br + ai * bi, ar * bi - ai * br], 0)


def turned(z):
    q = z.shape[0] // 4
    return jnp.concatenate([z[2 * q : 3 * q], -z[3 * q :], -z[:q], z[q : 2 * q]], 0)


def add_turned(y, z):
    q = z.shape[0] // 4
    return jnp.concatenate(
        [
            y[:q] + z[2 * q : 3 * q],
            y[q : 2 * q] - z[3 * q :],
            y[2 * q : 3 * q] - z[:q],
            y[3 * q :] + z[q : 2 * q],
        ],
        0,
    )


def conj_turned(w, z):
    n = w.shape[0] // 2
    h = n // 2
    wr, wi, zr, zi = w[:n], w[n:], z[:n], z[n:]
    re = wr * zi - wi * zr
    im = wr * zr + wi * zi
    return jnp.concatenate([re[:h], -re[h:], -im[:h], im[h:]], 0)


def kernel(
    size, factor,
    q1_in, k1_in, v1_in, q2_in, k2_in, co_in, taps_in, rates, res_in, tf_in, th_in, tn_in, ti_in,
    gq1, gk1, gv1, gq2, gk2, taps_st, res_st,
    q1, k1, v1, q2, k2, co, taps, res, tf, thr, thf, tn, ti,
    rise_t, ms_t, mst_t, lead_t, tail_t,
    lspec, kback, tspec, fspec, wone, mr_one, lback, ctail,
    bstate, bpeer, bsum, bslots, fstate, fpeer, fsum, fslots, halo_k, halo_v, chead, cnext, via_k, via_v, via_c,
    part, xch, got, gat, sib,
    in_sem, bp_send, bp_recv, bs_send, bs_recv, fp_send, fp_recv, fs_send, fs_recv,
    hf_send, hf_recv, hb_send, hb_recv, vf_send, vf_recv, vb_send, vb_recv,
    x_send, x_recv, r_send, r_recv, g_send, g_recv, s_send, s_recv,
):
    length, channels = q1.shape
    ntaps = taps.shape[0]
    modes = res.shape[0]
    groups = channels // (2 * WIDE)
    chips = size // 2
    slots = part.shape[2]
    lanes = WIDE // 128
    me = lax.axis_index("ctx")
    core, chip = lax.rem(me, 2), me // 2
    peer = me + 1 - 2 * core

    barrier = pltpu.get_barrier_semaphore()
    for k in range(1, size):
        pl.semaphore_signal(
            barrier, inc=1, device_id={"ctx": lax.rem(me + k, size)},
            device_id_type=pl.DeviceIdType.MESH,
        )

    loads = []
    for n, (src, dst) in enumerate(
        [
            (q2_in, q2), (co_in, co), (th_in, thr.at[pl.ds(0, 2 * ntaps)]), (th_in, thf.at[pl.ds(0, 2 * ntaps)]),
            (tn_in, tn), (res_in, res), (taps_in, taps), (tf_in, tf), (ti_in, ti),
            (k1_in, k1), (v1_in, v1), (q1_in, q1), (k2_in, k2),
        ]
    ):
        copy = pltpu.make_async_copy(src, dst, in_sem.at[n])
        copy.start()
        loads.append(copy)

    def remote(src, dst, send, recv, target):
        return pltpu.make_async_remote_copy(
            src_ref=src, dst_ref=dst, send_sem=send, recv_sem=recv,
            device_id={"ctx": target}, device_id_type=pl.DeviceIdType.MESH,
        )

    def wide_cols(g):
        return pl.ds(pl.multiple_of(g * 2 * WIDE, 2 * WIDE), 2 * WIDE)

    def rate_at(shape, dim):
        at = lax.rem(lax.broadcasted_iota(jnp.int32, shape, dim), modes)
        out = jnp.zeros(shape, f32)
        for m in range(modes):
            out = jnp.where(at == m, rates[m], out)
        return out

    def scale_of(rate):
        x = 2.0 * rate
        tail = 1.0 - x * (1.0 / 8.0)
        for n in range(7, 1, -1):
            tail = 1.0 - x * (1.0 / n) * tail
        return jnp.sqrt(x * tail)

    def iota(shape, dim):
        return lax.broadcasted_iota(jnp.int32, shape, dim)

    def first_rows(x):
        return jnp.where(iota(x.shape, 0) < modes, x, 0.0)

    def lane_parts(x):
        hi = x.astype(bf16).astype(f32)
        at = iota(x.shape, 1) // modes
        return jnp.where(at < 2, hi, jnp.where(at == 2, x - hi, 0.0)).astype(bf16)

    rows_long = rate_at((2 * modes, length), 0)
    places = iota((2 * modes, length), 1).astype(f32)
    rise_t[...] = three_lanes(first_rows(jnp.exp(-rows_long * places)))

    @pl.when(me == 0)
    def _():
        halo_k[...] = jnp.zeros_like(halo_k)
        halo_v[...] = jnp.zeros_like(halo_v)

    @pl.when(me == size - 1)
    def _():
        cnext[...] = jnp.zeros_like(cnext)

    @pl.when(core == 0)
    def _():
        fpeer[...] = jnp.zeros_like(fpeer)

    @pl.when(core == 1)
    def _():
        bpeer[...] = jnp.zeros_like(bpeer)

    for j in range(1, chips):
        @pl.when(chip + j >= chips)
        def _():
            bslots[j - 1] = jnp.zeros_like(bstate)

        @pl.when(chip - j < 0)
        def _():
            fslots[:, j - 1] = jnp.zeros((groups, modes, 2 * WIDE), f32)

    if part.shape[2] > (ntaps + modes) // 8 * lanes:
        used = (ntaps + modes) // 8 * lanes
        part[:, :, used:] = jnp.zeros((groups, 2, slots - used, 8, 128), f32)

    loads[0].wait()
    loads[1].wait()

    def first(g, carry):
        at = wide_cols(g)
        cotan = co[:, at].astype(f32) * q2[:, at].astype(f32)
        bstate[:, at] = dot(rise_t[...], three(cotan))[:modes]
        return carry

    lax.fori_loop(0, groups, first, 0)
    pl.semaphore_wait(barrier, size - 1)

    def back_peer():
        return remote(bstate, bpeer, bp_send, bp_recv, peer)

    def back_state(j, q, other):
        return remote(bsum, bslots.at[j - 1], bs_send.at[j - 1, q], bs_recv.at[j - 1], 2 * other + q)

    @pl.when(core == 1)
    def _():
        back_peer().start()

    low_mid, high_mid, detour = size // 2 - 1, size // 2, chips == 4

    def halo_copies(g, target):
        rows = pl.ds(length - ntaps, ntaps)
        return (
            remote(k1_in.at[rows, wide_cols(g)], halo_k.at[g], hf_send.at[0, g], hf_recv.at[0, g], target),
            remote(v1_in.at[rows, wide_cols(g)], halo_v.at[g], hf_send.at[1, g], hf_recv.at[1, g], target),
        )

    def halo_relay(g):
        rows = pl.ds(length - ntaps, ntaps)
        return (
            remote(k1_in.at[rows, wide_cols(g)], via_k.at[g], hf_send.at[0, g], vf_recv.at[0, g], size - 1),
            remote(v1_in.at[rows, wide_cols(g)], via_v.at[g], hf_send.at[1, g], vf_recv.at[1, g], size - 1),
        )

    def halo_relay_on(g):
        return (
            remote(via_k.at[g], halo_k.at[g], vf_send.at[0, g], hf_recv.at[0, g], high_mid),
            remote(via_v.at[g], halo_v.at[g], vf_send.at[1, g], hf_recv.at[1, g], high_mid),
        )

    def pass_halo(g):
        for copy in halo_relay(g):
            copy.wait_recv()
        for copy in halo_relay_on(g):
            copy.start()

    for g in range(groups):
        around = detour and g % 2 == 1

        @pl.when((me + 1 < size) & (me != low_mid) if around else me + 1 < size)
        def _():
            for copy in halo_copies(g, me + 1):
                copy.start()

        if around:
            @pl.when(me == low_mid)
            def _():
                for copy in halo_relay(g):
                    copy.start()

    for copy in loads[2:5]:
        copy.wait()

    rows_short = rate_at((2 * modes, ntaps), 0)
    places = iota((2 * modes, ntaps), 1).astype(f32)
    thr[2 * ntaps :] = three_lanes(first_rows(jnp.exp(-rows_short * places)))
    thf[2 * ntaps :] = three_lanes(first_rows(jnp.exp(-rows_short * (ntaps - 1.0 - places))))
    scaled = first_rows(scale_of(rows_short) * jnp.exp(-rows_short * places))
    back_table = jnp.concatenate(
        [tn[:, : 2 * ntaps], tn[:, 4 * ntaps :], tn[:, : 2 * ntaps]], 0
    )
    unit = 1.0 / ntaps
    mst_t[...] = three_lanes((unit * factor) * dot(three_lanes(scaled), back_table))
    lane_rate = rate_at((ntaps, 4 * modes), 1)
    places = iota((ntaps, 4 * modes), 0).astype(f32)
    lane_scale = scale_of(lane_rate)
    spread = dot(thr[: 2 * ntaps], three(lane_scale * jnp.exp(-lane_rate * places)))
    ms_t[...] = lane_parts(unit * spread)
    tail_t[...] = lane_parts(lane_scale * jnp.exp(-lane_rate * (ntaps - places)))
    lead_t[...] = lane_parts(lane_scale * jnp.exp(-lane_rate * (places + 1.0)))
    mode_rate = rate_at((modes, 2 * WIDE), 0)
    over_block = jnp.exp(-mode_rate * float(ntaps))
    over_device = jnp.exp(-mode_rate * float(length))
    over_chip = jnp.exp(-mode_rate * float(2 * length))

    @pl.when(core == 0)
    def _():
        back_peer().wait_recv()
        for g in range(groups):
            at = slice(2 * WIDE * g, 2 * WIDE * (g + 1))
            bsum[:, at] = bstate[:, at] + over_device * bpeer[:, at]
        for j in range(1, chips):
            @pl.when(chip - j >= 0)
            def _():
                for q in range(2):
                    back_state(j, q, chip - j).start()

    one_step = (factor * scale_of(mode_rate)) * jnp.exp(-mode_rate)
    nblocks = length // ntaps
    spec = 2 * ntaps

    blocks = [slice(b * ntaps, (b + 1) * ntaps) for b in range(nblocks)]
    across = 2 * WIDE

    def beside(arrays):
        return jnp.concatenate(arrays, 1)

    def apart(array):
        return [array[:, i : i + across] for i in range(0, array.shape[1], across)]

    def second(g, carry):
        at = wide_cols(g)
        cotan = co[:, at].astype(f32) * q2[:, at].astype(f32)
        mixed = k1[:, at].astype(f32) * v1[:, at].astype(f32)
        w = dot(tf[...], three(mixed))
        wone[:, at] = w
        fs = dot(ms_t[...], three_small(res[:, at]))
        fspec[:, at] = fs
        both = apart(dot(thr[...], beside([three(cotan[rows]) for rows in blocks] + [three(taps[:, at] * unit)])))
        ts = both[nblocks][:spec]
        tspec[:, at] = ts
        for b in range(nblocks):
            lspec[b, :, at] = both[b][:spec]
            kback[b, :, at] = both[b][spec : spec + modes]
        mr_one[:, at] = dot(ti[...], three(cmul(ts, w)))
        near = apart(dot(tn[...], beside([three(cmul_conj(fs, both[b][:spec])) for b in range(nblocks)])))
        for b in range(nblocks):
            lback[blocks[b], at] = near[b]
        return carry

    for copy in loads[5:]:
        copy.wait()

    ahead = min(2, groups)
    lax.fori_loop(0, ahead, second, 0)

    if detour and groups > 1:
        @pl.when(me == size - 1)
        def _():
            pass_halo(1)

    for j in range(1, chips):
        @pl.when(chip + j < chips)
        def _():
            back_state(j, core, chip + j).wait_recv()

    def cot_copy(g, target):
        return remote(chead.at[g], cnext.at[g], hb_send.at[g], hb_recv.at[g], target)

    def cot_relay(g):
        return remote(chead.at[g], via_c.at[g], hb_send.at[g], vb_recv.at[g], 0)

    def cot_relay_on(g):
        return remote(via_c.at[g], cnext.at[g], vb_send.at[g], hb_recv.at[g], low_mid)

    def cot_around(g):
        return (me == high_mid) & (lax.rem(g, 2) == 0) & (g + 1 < groups)

    def front_peer(g):
        return remote(fstate.at[g], fpeer.at[g], fp_send.at[g], fp_recv.at[g], peer)

    def front_copy(g, j, q, other):
        return remote(
            fsum.at[g], fslots.at[g, j - 1], fs_send.at[g, j - 1, q], fs_recv.at[g, j - 1], 2 * other + q
        )

    def front_out(g):
        @pl.when(core == 1)
        def _():
            front_peer(g).wait_recv()
            fsum[g] = over_device * fpeer[g] + fstate[g]
            for j in range(1, chips):
                @pl.when(chip + j < chips)
                def _():
                    for q in range(2):
                        front_copy(g, j, q, chip + j).start()

    def third(g):
        at = wide_cols(g)
        r = res[:, at]
        ts = tspec[:, at]
        cotan = co[:, at].astype(f32)
        key_li, query = k2[:, at].astype(f32), q1[:, at].astype(f32)
        state = bslots[chips - 2, :, at]
        for j in range(chips - 2, 0, -1):
            state = over_chip * state + bslots[j - 1, :, at]
        state = jnp.where(core == 0, bpeer[:, at] + over_device * state, state)
        later = [over_block * state + kback[1, :, at], state]
        far = apart(dot(tail_t[...], beside([three_small(r * later[b]) for b in range(nblocks)])))
        prior = halo_k[g].astype(f32) * halo_v[g].astype(f32)
        mixed = k1[:ntaps, at].astype(f32) * v1[:ntaps, at].astype(f32)
        w0 = dot(tf[...], three(jnp.concatenate([prior, mixed], 0)))
        back = lback[:, at] + jnp.concatenate(far, 0)
        mr_grad = cotan + key_li * back
        grad = mr_grad * query
        hi, lo = split(grad)
        chead[g, 0] = hi[:ntaps]
        chead[g, 1] = lo[:ntaps]

        if detour:
            @pl.when(cot_around(g))
            def _():
                cot_relay(g).start()

            @pl.when((me > 0) & jnp.logical_not(cot_around(g)))
            def _():
                cot_copy(g, me - 1).start()
        else:
            @pl.when(me > 0)
            def _():
                cot_copy(g, me - 1).start()

        mr0 = dot(ti[...], three(cmul(ts, w0)))
        cs = apart(dot(thr[:spec], beside([jnp.concatenate([hi[rows], lo[rows], hi[rows]], 0) for rows in blocks])))
        ctail[:, at] = cs[1]
        w1 = wone[:, at]
        mr = jnp.concatenate([mr0, mr_one[:, at]], 0)
        gq1[:, at] = (mr_grad * mr).astype(bf16)
        mr_out = query * mr
        gk2[:, at] = (mr_out * back).astype(bf16)
        x = key_li * mr_out
        both = apart(dot(thf[...], beside([three(x[rows]) for rows in blocks])))
        turn = conj_turned(w0, cs[0]) + conj_turned(w1, cs[1])
        taps_part = dot(tn[...], three(turn)) * (unit * factor)
        wone[:, at] = add_turned(cs[0], cs[1])
        for p in range(2):
            for i in range(ntaps // 8):
                for j in range(lanes):
                    lane = p * WIDE + 128 * j
                    part[g, p, i * lanes + j] = taps_part[8 * i : 8 * i + 8, lane : lane + 128]
        fronts = [both[b][spec : spec + modes] for b in range(nblocks)]
        fstate[g] = over_block * fronts[0] + fronts[1]
        lag = cmul_conj(both[0][:spec], lspec[0, :, at]) + cmul_conj(both[1][:spec], lspec[1, :, at])
        for b in range(nblocks):
            lspec[b, :, at] = both[b][:spec]
        kback[0, :, at] = fronts[0]
        res_part = dot(mst_t[...], three(lag))[:modes]
        res_part = res_part + one_step * (fronts[0] * later[0] + fronts[1] * later[1])
        for p in range(2):
            for j in range(lanes):
                lane = p * WIDE + 128 * j
                part[g, p, ntaps // 8 * lanes + j] = res_part[:, lane : lane + 128]

    def fourth(g):
        at = wide_cols(g)
        state = fslots[g, chips - 2]
        for j in range(chips - 2, 0, -1):
            state = over_chip * state + fslots[g, j - 1]
        state = jnp.where(core == 1, fpeer[g] + over_device * state, state)
        hi, lo = cnext[g, 0], cnext[g, 1]
        nxt = dot(thr[:spec], jnp.concatenate([hi, lo, hi], 0))
        r, ts, fs = res[:, at], tspec[:, at], fspec[:, at]
        before = [state, over_block * state + kback[0, :, at]]
        far = apart(dot(lead_t[...], beside([three_small(r * before[b]) for b in range(nblocks)])))
        spectra = [cmul(fs, lspec[b, :, at]) for b in range(nblocks)]
        spectra += [cmul_conj(ts, wone[:, at]), cmul_conj(ts, add_turned(ctail[:, at], nxt))]
        near = apart(dot(tn[...], beside([three(y) for y in spectra])))
        for b in range(nblocks):
            rows = blocks[b]
            gq2[rows, at] = (co[rows, at].astype(f32) * (near[b] + far[b])).astype(bf16)
            mg = near[nblocks + b]
            gk1[rows, at] = (mg * v1[rows, at].astype(f32)).astype(bf16)
            gv1[rows, at] = (mg * k1[rows, at].astype(f32)).astype(bf16)

    def to_peer(g):
        return remote(part.at[g, 1 - core], xch.at[g], x_send.at[g], x_recv.at[g], peer)

    share = slots // chips

    def after(j):
        return lax.rem(chip + j, chips)

    def before(j):
        return lax.rem(chip + chips - j, chips)

    def mine(owner):
        return pl.ds(owner * share, share)

    def scatter(g, j, other):
        return remote(
            part.at[g, core, mine(other)], got.at[g, pl.ds((j - 1) * share, share)],
            r_send.at[g, j - 1], r_recv.at[g, j - 1], 2 * other + core,
        )

    def gather(g, j, other, owner):
        return remote(
            gat.at[g, mine(owner)], gat.at[g, mine(owner)],
            g_send.at[g, j - 1], g_recv.at[g, j - 1], 2 * other + core,
        )

    def to_sib(g):
        return remote(gat.at[g], sib.at[g], s_send.at[g], s_recv.at[g], peer)

    def stage_peer(g):
        to_peer(g).wait_recv()
        part[g, core] = part[g, core] + xch[g]
        for j in range(1, chips):
            scatter(g, j, after(j)).start()
        front_out(g)

    def stage_scatter(g):
        total = part[g, core, mine(chip)]
        for j in range(1, chips):
            scatter(g, j, before(j)).wait_recv()
            total = total + got[g, pl.ds((j - 1) * share, share)]
        gat[g, mine(chip)] = total
        for j in range(1, chips):
            gather(g, j, after(j), chip).start()

    def stage_gather(g):
        for j in range(1, chips):
            gather(g, j, before(j), before(j)).wait_recv()
        to_sib(g).start()

    def stage_last(g):
        to_sib(g).wait_recv()
        for src, half in ((gat, core), (sib, 1 - core)):
            for j in range(lanes):
                at = pl.ds(pl.multiple_of((2 * g + half) * WIDE + 128 * j, 128), 128)
                for i in range(ntaps // 8):
                    taps_st[8 * i : 8 * i + 8, at] = src[g, i * lanes + j]
                res_st[:, at] = src[g, ntaps // 8 * lanes + j]

    ordered = ((1, stage_peer), (3, stage_scatter), (5, stage_gather), (6, stage_last))

    def stages(s):
        for lag, stage in ordered:
            g = s - lag

            @pl.when((g >= 0) & (g < groups))
            def _():
                stage(g)

    def third_group(g, carry):
        @pl.when(me > 0)
        def _():
            for copy in halo_copies(g, me - 1):
                copy.wait_recv()

        third(g)
        to_peer(g).start()

        @pl.when(core == 0)
        def _():
            front_peer(g).start()

        if detour:
            @pl.when((me == 0) & (lax.rem(g, 2) == 1))
            def _():
                cot_relay(g - 1).wait_recv()
                cot_relay_on(g - 1).start()

            @pl.when((me == size - 1) & (lax.rem(g, 2) == 0) & (g + 3 < groups))
            def _():
                pass_halo(g + 3)

        stages(g)

        @pl.when(g + ahead < groups)
        def _():
            second(g + ahead, 0)

        return carry

    lax.fori_loop(0, groups, third_group, 0)

    def fourth_group(s, carry):
        g = s - groups

        @pl.when(g < groups)
        def _():
            for j in range(1, chips):
                @pl.when(chip - j >= 0)
                def _():
                    front_copy(g, j, core, chip - j).wait_recv()

            @pl.when(me + 1 < size)
            def _():
                cot_copy(g, me + 1).wait_recv()

            fourth(g)

        stages(s)
        return carry

    lax.fori_loop(groups, groups + max(groups, ordered[-1][0]), fourth_group, 0)

    @pl.when(core == 1)
    def _():
        back_peer().wait_send()

    for j in range(1, chips):
        @pl.when((core == 0) & (chip - j >= 0))
        def _():
            for q in range(2):
                back_state(j, q, chip - j).wait_send()

    def finish(g, carry):
        odd = lax.rem(g, 2) == 1

        @pl.when(me + 1 < size)
        def _():
            for copy in halo_copies(g, me + 1):
                copy.wait_send()

        @pl.when(me > 0)
        def _():
            cot_copy(g, me - 1).wait_send()

        if detour:
            @pl.when((me == size - 1) & odd)
            def _():
                for copy in halo_relay_on(g):
                    copy.wait_send()

            @pl.when((me == 0) & jnp.logical_not(odd) & (g + 1 < groups))
            def _():
                cot_relay_on(g).wait_send()

        @pl.when(core == 0)
        def _():
            front_peer(g).wait_send()

        for j in range(1, chips):
            @pl.when((core == 1) & (chip + j < chips))
            def _():
                for q in range(2):
                    front_copy(g, j, q, chip + j).wait_send()

        to_peer(g).wait_send()
        to_sib(g).wait_send()
        for j in range(1, chips):
            scatter(g, j, after(j)).wait_send()
            gather(g, j, after(j), chip).wait_send()
        return carry

    lax.fori_loop(0, groups, finish, 0)


def write_out(*refs):
    copies = [pltpu.make_async_copy(refs[i], refs[7 + i], refs[14].at[i]) for i in range(7)]
    for copy in copies:
        copy.start()
    for copy in copies:
        copy.wait()


def per_device(q1, k1, v1, q2, k2, co, mr_taps, decay_rates, residues):
    size = lax.axis_size("ctx")
    length, channels = q1.shape
    ntaps, modes = mr_taps.shape[0], residues.shape[0]
    groups, chips = channels // (2 * WIDE), size // 2
    nblocks, spec = length // ntaps, 2 * ntaps
    used = (ntaps + modes) // 8 * (WIDE // 128)
    share = -(-used // chips)
    slots = share * chips
    factor = 1.0 / math.sqrt(length * size)
    consts = [jnp.asarray(t) for t in tables(ntaps)]

    def vm(*shape, dtype=f32):
        return pltpu.VMEM(shape, dtype)

    dma = lambda *shape: pltpu.SemaphoreType.DMA(shape)
    wide = lambda: vm(length, channels, dtype=bf16)
    scratch = [
        wide(), wide(), wide(), wide(), wide(), wide(),
        vm(ntaps, channels), vm(modes, channels),
        vm(spec, 3 * spec, dtype=bf16), vm(spec + 2 * modes, 3 * ntaps, dtype=bf16),
        vm(spec + 2 * modes, 3 * ntaps, dtype=bf16),
        vm(ntaps, 3 * spec, dtype=bf16), vm(ntaps, 3 * spec, dtype=bf16),
        vm(2 * modes, 3 * length, dtype=bf16), vm(spec, 4 * modes, dtype=bf16),
        vm(2 * modes, 3 * spec, dtype=bf16), vm(ntaps, 4 * modes, dtype=bf16),
        vm(ntaps, 4 * modes, dtype=bf16),
        vm(nblocks, spec, channels), vm(nblocks, modes, channels), vm(spec, channels), vm(spec, channels),
        vm(spec, channels), vm(ntaps, channels), vm(length, channels),
        vm(spec, channels),
        vm(modes, channels), vm(modes, channels), vm(modes, channels), vm(chips - 1, modes, channels),
        vm(groups, modes, 2 * WIDE), vm(groups, modes, 2 * WIDE), vm(groups, modes, 2 * WIDE),
        vm(groups, chips - 1, modes, 2 * WIDE),
        vm(groups, ntaps, 2 * WIDE, dtype=bf16), vm(groups, ntaps, 2 * WIDE, dtype=bf16),
        vm(groups, 2, ntaps, 2 * WIDE, dtype=bf16), vm(groups, 2, ntaps, 2 * WIDE, dtype=bf16),
        vm(groups, ntaps, 2 * WIDE, dtype=bf16), vm(groups, ntaps, 2 * WIDE, dtype=bf16),
        vm(groups, 2, ntaps, 2 * WIDE, dtype=bf16),
        vm(groups, 2, slots, 8, 128), vm(groups, slots, 8, 128), vm(groups, slots, 8, 128),
        vm(groups, slots, 8, 128), vm(groups, slots, 8, 128),
        dma(13), pltpu.SemaphoreType.DMA, pltpu.SemaphoreType.DMA, dma(chips - 1, 2), dma(chips - 1),
        dma(groups), dma(groups), dma(groups, chips - 1, 2), dma(groups, chips - 1),
        dma(2, groups), dma(2, groups), dma(groups), dma(groups),
        dma(2, groups), dma(2, groups), dma(groups), dma(groups),
        dma(groups), dma(groups), dma(groups, chips - 1), dma(groups, chips - 1),
        dma(groups, chips - 1), dma(groups, chips - 1), dma(groups), dma(groups),
    ]
    anywhere = pl.BlockSpec(memory_space=pl.ANY)
    specs = [anywhere] * 7 + [pl.BlockSpec(memory_space=pltpu.SMEM)] + [anywhere] * 5
    results = [((length, channels), bf16)] * 5 + [((ntaps, channels), f32), ((modes, channels), f32)]
    held = pl.pallas_call(
        lambda *refs: kernel(size, factor, *refs),
        out_shape=tuple(pltpu.VMEM(*r) for r in results),
        in_specs=specs,
        out_specs=(pl.BlockSpec(memory_space=pltpu.VMEM),) * 7,
        scratch_shapes=scratch,
        compiler_params=pltpu.CompilerParams(
            collective_id=0, has_side_effects=True, vmem_limit_bytes=50 * 2**20
        ),
        name="backward",
    )(q1, k1, v1, q2, k2, co, mr_taps, decay_rates, residues, *consts)
    held = [pltpu.with_memory_space_constraint(x, pltpu.VMEM) for x in held]
    return pl.pallas_call(
        write_out,
        out_shape=tuple(jax.ShapeDtypeStruct(*r) for r in results),
        in_specs=(pl.BlockSpec(memory_space=pltpu.VMEM),) * 7,
        out_specs=(anywhere,) * 7,
        scratch_shapes=[dma(7)],
        compiler_params=pltpu.CompilerParams(vmem_limit_bytes=2**20),
        name="write_out",
    )(*held)


def solution(mesh):
    whole, cols = P("ctx", "tp"), P(None, "tp")
    return jax.shard_map(
        per_device,
        mesh=mesh,
        in_specs=(whole,) * 6 + (cols, P(), cols),
        out_specs=(whole,) * 5 + (cols, cols),
        check_vma=False,
    )
```

```python
import math

import numpy as np
import ml_dtypes
import jax
import jax.numpy as jnp
from jax import lax
from jax.experimental import pallas as pl
from jax.experimental.pallas import tpu as pltpu
from jax.sharding import PartitionSpec as P

f32, bf16 = jnp.float32, jnp.bfloat16
WIDE = 256


def tables(taps):
    size, half = 2 * taps, taps // 2
    order = np.concatenate([np.arange(0, taps, 2), np.arange(1, taps, 2)])
    angle = (2.0 * np.pi / size) * (order[:, None] + 0.5) * np.arange(size)[None, :]
    full = np.concatenate([np.cos(angle), -np.sin(angle)], 0)

    def three(table):
        hi = table.astype(ml_dtypes.bfloat16)
        lo = (table - hi.astype(np.float64)).astype(ml_dtypes.bfloat16)
        return np.concatenate([hi, hi, lo], 1)

    return (
        three(full),
        three(full[:, :taps]),
        three(full[:, :taps].T),
        three(full[:, taps:].T),
    )


def split(x):
    hi = x.astype(bf16)
    return hi, (x - hi.astype(f32)).astype(bf16)


def three(x):
    hi, lo = split(x)
    return jnp.concatenate([hi, lo, hi], 0)


def three_small(x):
    hi = x.astype(bf16).astype(f32)
    return jnp.concatenate([hi, x - hi, hi, jnp.zeros_like(x)], 0).astype(bf16)


def three_lanes(x):
    hi, lo = split(x)
    return jnp.concatenate([hi, hi, lo], 1)


def dot(a, b):
    return jnp.dot(a, b, preferred_element_type=f32)


def parts_of(z):
    n = z.shape[0] // 2
    return z[:n], z[n:]


def cmul(a, b):
    (ar, ai), (br, bi) = parts_of(a), parts_of(b)
    return jnp.concatenate([ar * br - ai * bi, ar * bi + ai * br], 0)


def cmul_conj(a, b):
    (ar, ai), (br, bi) = parts_of(a), parts_of(b)
    return jnp.concatenate([ar * br + ai * bi, ar * bi - ai * br], 0)


def turned(z):
    q = z.shape[0] // 4
    return jnp.concatenate([z[2 * q : 3 * q], -z[3 * q :], -z[:q], z[q : 2 * q]], 0)


def add_turned(y, z):
    q = z.shape[0] // 4
    return jnp.concatenate(
        [
            y[:q] + z[2 * q : 3 * q],
            y[q : 2 * q] - z[3 * q :],
            y[2 * q : 3 * q] - z[:q],
            y[3 * q :] + z[q : 2 * q],
        ],
        0,
    )


def conj_turned(w, z):
    n = w.shape[0] // 2
    h = n // 2
    wr, wi, zr, zi = w[:n], w[n:], z[:n], z[n:]
    re = wr * zi - wi * zr
    im = wr * zr + wi * zi
    return jnp.concatenate([re[:h], -re[h:], -im[:h], im[h:]], 0)


def kernel(
    size, factor,
    q1_in, k1_in, v1_in, q2_in, k2_in, co_in, taps_in, rates, res_in, tf_in, th_in, tn_in, ti_in,
    gq1, gk1, gv1, gq2, gk2, taps_st, res_st,
    q1, k1, v1, q2, k2, co, taps, res, tf, thr, thf, tn, ti,
    rise_t, ms_t, mst_t, lead_t, tail_t,
    lspec, kback, tspec, fspec, wone, mr_one, lback, ctail,
    bstate, bpeer, bsum, bslots, fstate, fpeer, fsum, fslots, halo_k, halo_v, chead, cnext, via_k, via_v, via_c,
    part, xch, got, gat, sib,
    in_sem, bp_send, bp_recv, bs_send, bs_recv, fp_send, fp_recv, fs_send, fs_recv,
    hf_send, hf_recv, hb_send, hb_recv, vf_send, vf_recv, vb_send, vb_recv,
    x_send, x_recv, r_send, r_recv, g_send, g_recv, s_send, s_recv,
):
    length, channels = q1.shape
    ntaps = taps.shape[0]
    modes = res.shape[0]
    groups = channels // (2 * WIDE)
    chips = size // 2
    slots = part.shape[2]
    lanes = WIDE // 128
    me = lax.axis_index("ctx")
    core, chip = lax.rem(me, 2), me // 2
    peer = me + 1 - 2 * core

    barrier = pltpu.get_barrier_semaphore()
    for k in range(1, size):
        pl.semaphore_signal(
            barrier, inc=1, device_id={"ctx": lax.rem(me + k, size)},
            device_id_type=pl.DeviceIdType.MESH,
        )

    loads = []
    for n, (src, dst) in enumerate(
        [
            (q2_in, q2), (co_in, co), (th_in, thr.at[pl.ds(0, 2 * ntaps)]), (th_in, thf.at[pl.ds(0, 2 * ntaps)]),
            (tn_in, tn), (res_in, res), (taps_in, taps), (tf_in, tf), (ti_in, ti),
            (k1_in, k1), (v1_in, v1), (q1_in, q1), (k2_in, k2),
        ]
    ):
        copy = pltpu.make_async_copy(src, dst, in_sem.at[n])
        copy.start()
        loads.append(copy)

    def remote(src, dst, send, recv, target):
        return pltpu.make_async_remote_copy(
            src_ref=src, dst_ref=dst, send_sem=send, recv_sem=recv,
            device_id={"ctx": target}, device_id_type=pl.DeviceIdType.MESH,
        )

    def wide_cols(g):
        return pl.ds(pl.multiple_of(g * 2 * WIDE, 2 * WIDE), 2 * WIDE)

    def rate_at(shape, dim):
        at = lax.rem(lax.broadcasted_iota(jnp.int32, shape, dim), modes)
        out = jnp.zeros(shape, f32)
        for m in range(modes):
            out = jnp.where(at == m, rates[m], out)
        return out

    def scale_of(rate):
        x = 2.0 * rate
        tail = 1.0 - x * (1.0 / 8.0)
        for n in range(7, 1, -1):
            tail = 1.0 - x * (1.0 / n) * tail
        return jnp.sqrt(x * tail)

    def iota(shape, dim):
        return lax.broadcasted_iota(jnp.int32, shape, dim)

    def first_rows(x):
        return jnp.where(iota(x.shape, 0) < modes, x, 0.0)

    def lane_parts(x):
        hi = x.astype(bf16).astype(f32)
        at = iota(x.shape, 1) // modes
        return jnp.where(at < 2, hi, jnp.where(at == 2, x - hi, 0.0)).astype(bf16)

    rows_long = rate_at((2 * modes, length), 0)
    places = iota((2 * modes, length), 1).astype(f32)
    rise_t[...] = three_lanes(first_rows(jnp.exp(-rows_long * places)))

    @pl.when(me == 0)
    def _():
        halo_k[...] = jnp.zeros_like(halo_k)
        halo_v[...] = jnp.zeros_like(halo_v)

    @pl.when(me == size - 1)
    def _():
        cnext[...] = jnp.zeros_like(cnext)

    @pl.when(core == 0)
    def _():
        fpeer[...] = jnp.zeros_like(fpeer)

    @pl.when(core == 1)
    def _():
        bpeer[...] = jnp.zeros_like(bpeer)

    for j in range(1, chips):
        @pl.when(chip + j >= chips)
        def _():
            bslots[j - 1] = jnp.zeros_like(bstate)

        @pl.when(chip - j < 0)
        def _():
            fslots[:, j - 1] = jnp.zeros((groups, modes, 2 * WIDE), f32)

    if part.shape[2] > (ntaps + modes) // 8 * lanes:
        used = (ntaps + modes) // 8 * lanes
        part[:, :, used:] = jnp.zeros((groups, 2, slots - used, 8, 128), f32)

    loads[0].wait()
    loads[1].wait()

    def first(g, carry):
        at = wide_cols(g)
        cotan = co[:, at].astype(f32) * q2[:, at].astype(f32)
        bstate[:, at] = dot(rise_t[...], three(cotan))[:modes]
        return carry

    lax.fori_loop(0, groups, first, 0)
    pl.semaphore_wait(barrier, size - 1)

    def back_peer():
        return remote(bstate, bpeer, bp_send, bp_recv, peer)

    def back_state(j, q, other):
        return remote(bsum, bslots.at[j - 1], bs_send.at[j - 1, q], bs_recv.at[j - 1], 2 * other + q)

    @pl.when(core == 1)
    def _():
        back_peer().start()

    low_mid, high_mid, detour = size // 2 - 1, size // 2, chips == 4

    def halo_copies(g, target):
        rows = pl.ds(length - ntaps, ntaps)
        return (
            remote(k1_in.at[rows, wide_cols(g)], halo_k.at[g], hf_send.at[0, g], hf_recv.at[0, g], target),
            remote(v1_in.at[rows, wide_cols(g)], halo_v.at[g], hf_send.at[1, g], hf_recv.at[1, g], target),
        )

    def halo_relay(g):
        rows = pl.ds(length - ntaps, ntaps)
        return (
            remote(k1_in.at[rows, wide_cols(g)], via_k.at[g], hf_send.at[0, g], vf_recv.at[0, g], size - 1),
            remote(v1_in.at[rows, wide_cols(g)], via_v.at[g], hf_send.at[1, g], vf_recv.at[1, g], size - 1),
        )

    def halo_relay_on(g):
        return (
            remote(via_k.at[g], halo_k.at[g], vf_send.at[0, g], hf_recv.at[0, g], high_mid),
            remote(via_v.at[g], halo_v.at[g], vf_send.at[1, g], hf_recv.at[1, g], high_mid),
        )

    def pass_halo(g):
        for copy in halo_relay(g):
            copy.wait_recv()
        for copy in halo_relay_on(g):
            copy.start()

    for g in range(groups):
        around = detour and g % 4 >= 2

        @pl.when((me + 1 < size) & (me != low_mid) if around else me + 1 < size)
        def _():
            for copy in halo_copies(g, me + 1):
                copy.start()

        if around:
            @pl.when(me == low_mid)
            def _():
                for copy in halo_relay(g):
                    copy.start()

    for copy in loads[2:5]:
        copy.wait()

    rows_short = rate_at((2 * modes, ntaps), 0)
    places = iota((2 * modes, ntaps), 1).astype(f32)
    thr[2 * ntaps :] = three_lanes(first_rows(jnp.exp(-rows_short * places)))
    thf[2 * ntaps :] = three_lanes(first_rows(jnp.exp(-rows_short * (ntaps - 1.0 - places))))
    scaled = first_rows(scale_of(rows_short) * jnp.exp(-rows_short * places))
    back_table = jnp.concatenate(
        [tn[:, : 2 * ntaps], tn[:, 4 * ntaps :], tn[:, : 2 * ntaps]], 0
    )
    unit = 1.0 / ntaps
    mst_t[...] = three_lanes((unit * factor) * dot(three_lanes(scaled), back_table))
    lane_rate = rate_at((ntaps, 4 * modes), 1)
    places = iota((ntaps, 4 * modes), 0).astype(f32)
    lane_scale = scale_of(lane_rate)
    spread = dot(thr[: 2 * ntaps], three(lane_scale * jnp.exp(-lane_rate * places)))
    ms_t[...] = lane_parts(unit * spread)
    tail_t[...] = lane_parts(lane_scale * jnp.exp(-lane_rate * (ntaps - places)))
    lead_t[...] = lane_parts(lane_scale * jnp.exp(-lane_rate * (places + 1.0)))
    mode_rate = rate_at((modes, 2 * WIDE), 0)
    over_block = jnp.exp(-mode_rate * float(ntaps))
    over_device = jnp.exp(-mode_rate * float(length))
    over_chip = jnp.exp(-mode_rate * float(2 * length))

    @pl.when(core == 0)
    def _():
        back_peer().wait_recv()
        for g in range(groups):
            at = slice(2 * WIDE * g, 2 * WIDE * (g + 1))
            bsum[:, at] = bstate[:, at] + over_device * bpeer[:, at]
        for j in range(1, chips):
            @pl.when(chip - j >= 0)
            def _():
                for q in range(2):
                    back_state(j, q, chip - j).start()

    one_step = (factor * scale_of(mode_rate)) * jnp.exp(-mode_rate)
    nblocks = length // ntaps
    spec = 2 * ntaps

    blocks = [slice(b * ntaps, (b + 1) * ntaps) for b in range(nblocks)]
    across = 2 * WIDE

    def beside(arrays):
        return jnp.concatenate(arrays, 1)

    def apart(array):
        return [array[:, i : i + across] for i in range(0, array.shape[1], across)]

    def second(g, carry):
        at = wide_cols(g)
        cotan = co[:, at].astype(f32) * q2[:, at].astype(f32)
        mixed = k1[:, at].astype(f32) * v1[:, at].astype(f32)
        w = dot(tf[...], three(mixed))
        wone[:, at] = w
        fs = dot(ms_t[...], three_small(res[:, at]))
        fspec[:, at] = fs
        both = apart(dot(thr[...], beside([three(cotan[rows]) for rows in blocks] + [three(taps[:, at] * unit)])))
        ts = both[nblocks][:spec]
        tspec[:, at] = ts
        for b in range(nblocks):
            lspec[b, :, at] = both[b][:spec]
            kback[b, :, at] = both[b][spec : spec + modes]
        mr_one[:, at] = dot(ti[...], three(cmul(ts, w)))
        near = apart(dot(tn[...], beside([three(cmul_conj(fs, both[b][:spec])) for b in range(nblocks)])))
        for b in range(nblocks):
            lback[blocks[b], at] = near[b]
        return carry

    for copy in loads[5:]:
        copy.wait()

    ahead = min(2, groups)
    lax.fori_loop(0, ahead, second, 0)


    for j in range(1, chips):
        @pl.when(chip + j < chips)
        def _():
            back_state(j, core, chip + j).wait_recv()

    def cot_copy(g, target):
        return remote(chead.at[g], cnext.at[g], hb_send.at[g], hb_recv.at[g], target)

    def cot_relay(g):
        return remote(chead.at[g], via_c.at[g], hb_send.at[g], vb_recv.at[g], 0)

    def cot_relay_on(g):
        return remote(via_c.at[g], cnext.at[g], vb_send.at[g], hb_recv.at[g], low_mid)

    def cot_around(g):
        return (me == high_mid) & (lax.rem(g, 2) == 0) & (g + 1 < groups)

    def front_peer(g):
        return remote(fstate.at[g], fpeer.at[g], fp_send.at[g], fp_recv.at[g], peer)

    def front_copy(g, j, q, other):
        return remote(
            fsum.at[g], fslots.at[g, j - 1], fs_send.at[g, j - 1, q], fs_recv.at[g, j - 1], 2 * other + q
        )

    def front_out(g):
        @pl.when(core == 1)
        def _():
            front_peer(g).wait_recv()
            fsum[g] = over_device * fpeer[g] + fstate[g]
            for j in range(1, chips):
                @pl.when(chip + j < chips)
                def _():
                    for q in range(2):
                        front_copy(g, j, q, chip + j).start()

    def third(g):
        at = wide_cols(g)
        r = res[:, at]
        ts = tspec[:, at]
        cotan = co[:, at].astype(f32)
        key_li, query = k2[:, at].astype(f32), q1[:, at].astype(f32)
        state = bslots[chips - 2, :, at]
        for j in range(chips - 2, 0, -1):
            state = over_chip * state + bslots[j - 1, :, at]
        state = jnp.where(core == 0, bpeer[:, at] + over_device * state, state)
        later = [over_block * state + kback[1, :, at], state]
        far = apart(dot(tail_t[...], beside([three_small(r * later[b]) for b in range(nblocks)])))
        prior = halo_k[g].astype(f32) * halo_v[g].astype(f32)
        mixed = k1[:ntaps, at].astype(f32) * v1[:ntaps, at].astype(f32)
        w0 = dot(tf[...], three(jnp.concatenate([prior, mixed], 0)))
        back = lback[:, at] + jnp.concatenate(far, 0)
        mr_grad = cotan + key_li * back
        grad = mr_grad * query
        hi, lo = split(grad)
        chead[g, 0] = hi[:ntaps]
        chead[g, 1] = lo[:ntaps]

        if detour:
            @pl.when(cot_around(g))
            def _():
                cot_relay(g).start()

            @pl.when((me > 0) & jnp.logical_not(cot_around(g)))
            def _():
                cot_copy(g, me - 1).start()
        else:
            @pl.when(me > 0)
            def _():
                cot_copy(g, me - 1).start()

        mr0 = dot(ti[...], three(cmul(ts, w0)))
        cs = apart(dot(thr[:spec], beside([jnp.concatenate([hi[rows], lo[rows], hi[rows]], 0) for rows in blocks])))
        ctail[:, at] = cs[1]
        w1 = wone[:, at]
        mr = jnp.concatenate([mr0, mr_one[:, at]], 0)
        gq1[:, at] = (mr_grad * mr).astype(bf16)
        mr_out = query * mr
        gk2[:, at] = (mr_out * back).astype(bf16)
        x = key_li * mr_out
        both = apart(dot(thf[...], beside([three(x[rows]) for rows in blocks])))
        turn = conj_turned(w0, cs[0]) + conj_turned(w1, cs[1])
        taps_part = dot(tn[...], three(turn)) * (unit * factor)
        wone[:, at] = add_turned(cs[0], cs[1])
        for p in range(2):
            for i in range(ntaps // 8):
                for j in range(lanes):
                    lane = p * WIDE + 128 * j
                    part[g, p, i * lanes + j] = taps_part[8 * i : 8 * i + 8, lane : lane + 128]
        fronts = [both[b][spec : spec + modes] for b in range(nblocks)]
        fstate[g] = over_block * fronts[0] + fronts[1]
        lag = cmul_conj(both[0][:spec], lspec[0, :, at]) + cmul_conj(both[1][:spec], lspec[1, :, at])
        for b in range(nblocks):
            lspec[b, :, at] = both[b][:spec]
        kback[0, :, at] = fronts[0]
        res_part = dot(mst_t[...], three(lag))[:modes]
        res_part = res_part + one_step * (fronts[0] * later[0] + fronts[1] * later[1])
        for p in range(2):
            for j in range(lanes):
                lane = p * WIDE + 128 * j
                part[g, p, ntaps // 8 * lanes + j] = res_part[:, lane : lane + 128]

    def fourth(g):
        at = wide_cols(g)
        state = fslots[g, chips - 2]
        for j in range(chips - 2, 0, -1):
            state = over_chip * state + fslots[g, j - 1]
        state = jnp.where(core == 1, fpeer[g] + over_device * state, state)
        hi, lo = cnext[g, 0], cnext[g, 1]
        nxt = dot(thr[:spec], jnp.concatenate([hi, lo, hi], 0))
        r, ts, fs = res[:, at], tspec[:, at], fspec[:, at]
        before = [state, over_block * state + kback[0, :, at]]
        far = apart(dot(lead_t[...], beside([three_small(r * before[b]) for b in range(nblocks)])))
        spectra = [cmul(fs, lspec[b, :, at]) for b in range(nblocks)]
        spectra += [cmul_conj(ts, wone[:, at]), cmul_conj(ts, add_turned(ctail[:, at], nxt))]
        near = apart(dot(tn[...], beside([three(y) for y in spectra])))
        for b in range(nblocks):
            rows = blocks[b]
            gq2[rows, at] = (co[rows, at].astype(f32) * (near[b] + far[b])).astype(bf16)
            mg = near[nblocks + b]
            gk1[rows, at] = (mg * v1[rows, at].astype(f32)).astype(bf16)
            gv1[rows, at] = (mg * k1[rows, at].astype(f32)).astype(bf16)

    def to_peer(g):
        return remote(part.at[g, 1 - core], xch.at[g], x_send.at[g], x_recv.at[g], peer)

    share = slots // chips

    def after(j):
        return lax.rem(chip + j, chips)

    def before(j):
        return lax.rem(chip + chips - j, chips)

    def mine(owner):
        return pl.ds(owner * share, share)

    def scatter(g, j, other):
        return remote(
            part.at[g, core, mine(other)], got.at[g, pl.ds((j - 1) * share, share)],
            r_send.at[g, j - 1], r_recv.at[g, j - 1], 2 * other + core,
        )

    def gather(g, j, other, owner):
        return remote(
            gat.at[g, mine(owner)], gat.at[g, mine(owner)],
            g_send.at[g, j - 1], g_recv.at[g, j - 1], 2 * other + core,
        )

    def to_sib(g):
        return remote(gat.at[g], sib.at[g], s_send.at[g], s_recv.at[g], peer)

    def stage_peer(g):
        to_peer(g).wait_recv()
        part[g, core] = part[g, core] + xch[g]
        for j in range(1, chips):
            scatter(g, j, after(j)).start()
        front_out(g)

    def stage_scatter(g):
        total = part[g, core, mine(chip)]
        for j in range(1, chips):
            scatter(g, j, before(j)).wait_recv()
            total = total + got[g, pl.ds((j - 1) * share, share)]
        gat[g, mine(chip)] = total
        for j in range(1, chips):
            gather(g, j, after(j), chip).start()

    def stage_gather(g):
        for j in range(1, chips):
            gather(g, j, before(j), before(j)).wait_recv()
        to_sib(g).start()

    def stage_last(g):
        to_sib(g).wait_recv()
        for src, half in ((gat, core), (sib, 1 - core)):
            for j in range(lanes):
                at = pl.ds(pl.multiple_of((2 * g + half) * WIDE + 128 * j, 128), 128)
                for i in range(ntaps // 8):
                    taps_st[8 * i : 8 * i + 8, at] = src[g, i * lanes + j]
                res_st[:, at] = src[g, ntaps // 8 * lanes + j]

    ordered = ((1, stage_peer), (3, stage_scatter), (5, stage_gather), (6, stage_last))

    def stages(s):
        for lag, stage in ordered:
            g = s - lag

            @pl.when((g >= 0) & (g < groups))
            def _():
                stage(g)

    def third_group(g, carry):
        @pl.when(me > 0)
        def _():
            for copy in halo_copies(g, me - 1):
                copy.wait_recv()

        third(g)
        to_peer(g).start()

        @pl.when(core == 0)
        def _():
            front_peer(g).start()

        if detour:
            @pl.when((me == 0) & (lax.rem(g, 2) == 1))
            def _():
                cot_relay(g - 1).wait_recv()
                cot_relay_on(g - 1).start()

            @pl.when((me == size - 1) & (lax.rem(g, 4) < 2) & (g + 2 < groups))
            def _():
                pass_halo(g + 2)

        stages(g)

        @pl.when(g + ahead < groups)
        def _():
            second(g + ahead, 0)

        return carry

    lax.fori_loop(0, groups, third_group, 0)

    def fourth_group(s, carry):
        g = s - groups

        @pl.when(g < groups)
        def _():
            for j in range(1, chips):
                @pl.when(chip - j >= 0)
                def _():
                    front_copy(g, j, core, chip - j).wait_recv()

            @pl.when(me + 1 < size)
            def _():
                cot_copy(g, me + 1).wait_recv()

            fourth(g)

        stages(s)
        return carry

    lax.fori_loop(groups, groups + max(groups, ordered[-1][0]), fourth_group, 0)

    @pl.when(core == 1)
    def _():
        back_peer().wait_send()

    for j in range(1, chips):
        @pl.when((core == 0) & (chip - j >= 0))
        def _():
            for q in range(2):
                back_state(j, q, chip - j).wait_send()

    def finish(g, carry):
        odd = lax.rem(g, 2) == 1

        @pl.when(me + 1 < size)
        def _():
            for copy in halo_copies(g, me + 1):
                copy.wait_send()

        @pl.when(me > 0)
        def _():
            cot_copy(g, me - 1).wait_send()

        if detour:
            @pl.when((me == size - 1) & (lax.rem(g, 4) >= 2))
            def _():
                for copy in halo_relay_on(g):
                    copy.wait_send()

            @pl.when((me == 0) & jnp.logical_not(odd) & (g + 1 < groups))
            def _():
                cot_relay_on(g).wait_send()

        @pl.when(core == 0)
        def _():
            front_peer(g).wait_send()

        for j in range(1, chips):
            @pl.when((core == 1) & (chip + j < chips))
            def _():
                for q in range(2):
                    front_copy(g, j, q, chip + j).wait_send()

        to_peer(g).wait_send()
        to_sib(g).wait_send()
        for j in range(1, chips):
            scatter(g, j, after(j)).wait_send()
            gather(g, j, after(j), chip).wait_send()
        return carry

    lax.fori_loop(0, groups, finish, 0)


def write_out(*refs):
    copies = [pltpu.make_async_copy(refs[i], refs[7 + i], refs[14].at[i]) for i in range(7)]
    for copy in copies:
        copy.start()
    for copy in copies:
        copy.wait()


def per_device(q1, k1, v1, q2, k2, co, mr_taps, decay_rates, residues):
    size = lax.axis_size("ctx")
    length, channels = q1.shape
    ntaps, modes = mr_taps.shape[0], residues.shape[0]
    groups, chips = channels // (2 * WIDE), size // 2
    nblocks, spec = length // ntaps, 2 * ntaps
    used = (ntaps + modes) // 8 * (WIDE // 128)
    share = -(-used // chips)
    slots = share * chips
    factor = 1.0 / math.sqrt(length * size)
    consts = [jnp.asarray(t) for t in tables(ntaps)]

    def vm(*shape, dtype=f32):
        return pltpu.VMEM(shape, dtype)

    dma = lambda *shape: pltpu.SemaphoreType.DMA(shape)
    wide = lambda: vm(length, channels, dtype=bf16)
    scratch = [
        wide(), wide(), wide(), wide(), wide(), wide(),
        vm(ntaps, channels), vm(modes, channels),
        vm(spec, 3 * spec, dtype=bf16), vm(spec + 2 * modes, 3 * ntaps, dtype=bf16),
        vm(spec + 2 * modes, 3 * ntaps, dtype=bf16),
        vm(ntaps, 3 * spec, dtype=bf16), vm(ntaps, 3 * spec, dtype=bf16),
        vm(2 * modes, 3 * length, dtype=bf16), vm(spec, 4 * modes, dtype=bf16),
        vm(2 * modes, 3 * spec, dtype=bf16), vm(ntaps, 4 * modes, dtype=bf16),
        vm(ntaps, 4 * modes, dtype=bf16),
        vm(nblocks, spec, channels), vm(nblocks, modes, channels), vm(spec, channels), vm(spec, channels),
        vm(spec, channels), vm(ntaps, channels), vm(length, channels),
        vm(spec, channels),
        vm(modes, channels), vm(modes, channels), vm(modes, channels), vm(chips - 1, modes, channels),
        vm(groups, modes, 2 * WIDE), vm(groups, modes, 2 * WIDE), vm(groups, modes, 2 * WIDE),
        vm(groups, chips - 1, modes, 2 * WIDE),
        vm(groups, ntaps, 2 * WIDE, dtype=bf16), vm(groups, ntaps, 2 * WIDE, dtype=bf16),
        vm(groups, 2, ntaps, 2 * WIDE, dtype=bf16), vm(groups, 2, ntaps, 2 * WIDE, dtype=bf16),
        vm(groups, ntaps, 2 * WIDE, dtype=bf16), vm(groups, ntaps, 2 * WIDE, dtype=bf16),
        vm(groups, 2, ntaps, 2 * WIDE, dtype=bf16),
        vm(groups, 2, slots, 8, 128), vm(groups, slots, 8, 128), vm(groups, slots, 8, 128),
        vm(groups, slots, 8, 128), vm(groups, slots, 8, 128),
        dma(13), pltpu.SemaphoreType.DMA, pltpu.SemaphoreType.DMA, dma(chips - 1, 2), dma(chips - 1),
        dma(groups), dma(groups), dma(groups, chips - 1, 2), dma(groups, chips - 1),
        dma(2, groups), dma(2, groups), dma(groups), dma(groups),
        dma(2, groups), dma(2, groups), dma(groups), dma(groups),
        dma(groups), dma(groups), dma(groups, chips - 1), dma(groups, chips - 1),
        dma(groups, chips - 1), dma(groups, chips - 1), dma(groups), dma(groups),
    ]
    anywhere = pl.BlockSpec(memory_space=pl.ANY)
    specs = [anywhere] * 7 + [pl.BlockSpec(memory_space=pltpu.SMEM)] + [anywhere] * 5
    results = [((length, channels), bf16)] * 5 + [((ntaps, channels), f32), ((modes, channels), f32)]
    held = pl.pallas_call(
        lambda *refs: kernel(size, factor, *refs),
        out_shape=tuple(pltpu.VMEM(*r) for r in results),
        in_specs=specs,
        out_specs=(pl.BlockSpec(memory_space=pltpu.VMEM),) * 7,
        scratch_shapes=scratch,
        compiler_params=pltpu.CompilerParams(
            collective_id=0, has_side_effects=True, vmem_limit_bytes=50 * 2**20
        ),
        name="backward",
    )(q1, k1, v1, q2, k2, co, mr_taps, decay_rates, residues, *consts)
    held = [pltpu.with_memory_space_constraint(x, pltpu.VMEM) for x in held]
    return pl.pallas_call(
        write_out,
        out_shape=tuple(jax.ShapeDtypeStruct(*r) for r in results),
        in_specs=(pl.BlockSpec(memory_space=pltpu.VMEM),) * 7,
        out_specs=(anywhere,) * 7,
        scratch_shapes=[dma(7)],
        compiler_params=pltpu.CompilerParams(vmem_limit_bytes=2**20),
        name="write_out",
    )(*held)


def solution(mesh):
    whole, cols = P("ctx", "tp"), P(None, "tp")
    return jax.shard_map(
        per_device,
        mesh=mesh,
        in_specs=(whole,) * 6 + (cols, P(), cols),
        out_specs=(whole,) * 5 + (cols, cols),
        check_vma=False,
    )
```
